32 devices in a mesh: dp: 2 (over x), expert: 16 (over z, y, core).
Axes of the slice: x: 2, y: 2, z: 4, core: 2. Of those that a mesh axis runs over, the one named last changes fastest.
Arguments:
- out_grad: bfloat16 [4096, 1040], P(('dp', 'expert')), may hold values from -8 to 8
- routes: int32 [4096, 1], P(('dp', 'expert')), may hold values from 0 to 15; in each aligned block of 128 rows (0 to 127, 128 to 255, ...) at most 12 rows name the same one
- pre_act: bfloat16 [6144, 3072], P(('dp', 'expert')), may hold values from -6 to 6
- out_weight: bfloat16 [16, 3072, 1040], P('expert', 'dp'), may hold values from -0.109375 to 0.109375
- row_factor: float32 [16, 3072], P('expert', 'dp'), may hold values from 1 to 100
- col_factor: float32 [16, 1040], P('expert'), may hold values from 1 to 100
Outputs:
- hidden_grad: bfloat16 [4096, 3072], P(('dp', 'expert'))
- new_weight: bfloat16 [16, 3072, 1040], P('expert', 'dp')
- new_row: float32 [16, 3072], P('expert', 'dp')
- new_col: float32 [16, 1040], P('expert')
The draws below stay inside these ranges and needn't reach their ends.
Inputs may be any that keep to these rules, and one draw needn't show every extreme that they name: `routes`: in the rows of one device no expert is named by more than 12 rows.
All inputs are finite; a program needn't handle non-finite values.
Results may differ from the reference program's by a relative error of at most 0.0025.
Values may be sent and summed in bfloat16 or wider, within the bound.
A program may use at most 64 MiB of HBM per device.

```python
import math
import jax
import jax.numpy as jnp
import numpy as np
from jax import lax

D = 1040
FF = 3072
TOK_DEV = 128
EXPERTS = 16
SLOT = 12
R = 192
TOKENS = 4096
N_DP = 2
N_EXPERT = 16


def draw_out_grad(key, part):
    key_scale, key_base = jax.random.split(jax.random.fold_in(key, 11))
    levels = jnp.exp(jax.random.uniform(key_scale, (N_DP, 1, D), jnp.float32, math.log(0.3), math.log(3.2)))
    base_value = jax.random.normal(key_base, (N_DP, TOKENS // N_DP, D), jnp.float32)
    shaped = jnp.clip(base_value * levels, -8.0, 8.0)
    return shaped.reshape(TOKENS, D).astype(jnp.bfloat16)


def draw_pre_act(key, part):
    slot_rows = N_EXPERT * R
    blocks = 64
    key_level, key_base = jax.random.split(jax.random.fold_in(key, 23), 2)
    levels = jnp.exp(jax.random.uniform(key_level, (N_DP, 1, blocks, 1), jnp.float32, -1.2 * math.log(10.0), 0.5 * math.log(10.0)))
    base_value = jax.random.normal(key_base, (N_DP, slot_rows, blocks, FF // blocks), jnp.float32)
    shaped = jnp.clip(base_value * levels, -6.0, 6.0)
    return shaped.reshape(N_DP * slot_rows, FF).astype(jnp.bfloat16)


def level_of(stream_key, extent, pieces, smallest, largest):
    def one(axis_at, parts):
        draws = jax.random.uniform(jax.random.fold_in(jax.random.fold_in(stream_key, 6), axis_at), (parts,), jnp.float32, smallest / len(pieces), largest / len(pieces))
        return jnp.repeat(jnp.exp(draws), extent[axis_at] // parts).reshape((-1,) + (1,) * (len(extent) - axis_at - 1))

    loudness = one(*pieces[0])
    for cut in pieces[1:]:
        loudness = loudness * one(*cut)
    return loudness


def routed_block(own_key, own, number, rows, amount, top, reach, slope):
    order = jax.random.permutation(own_key, amount)
    heavy_load, ordinary = shares(amount, rows * top, reach, slope, True), shares(amount, rows * top, reach, slope, False)
    places = jnp.arange(amount)

    def named(lengths, rotation):
        used = int((lengths > 0).sum())
        fixed = max(1, used // 4)
        moved = fixed + (places - fixed + rotation * (used - fixed)) % max(1, amount - fixed)
        return jnp.zeros((amount,), jnp.int32).at[order[jnp.where(places < fixed, places, moved)]].set(jnp.asarray(lengths, jnp.int32))

    lengths = jnp.where(number % 4 == 0, named(heavy_load, number // 4), named(ordinary, number - number // 4 - 1))
    mixed = jax.random.permutation(jax.random.fold_in(own, 3), amount)
    source_of, taker = mixed[0:amount // 2 * 2:2], mixed[1:amount // 2 * 2:2]
    room = jnp.minimum(lengths[source_of] - 1, reach - lengths[taker]) // 2
    room = jnp.where((source_of == order[0]) | (taker == order[0]) | (lengths[taker] == 0), 0, jnp.maximum(room, 0))
    moved = jax.random.randint(jax.random.fold_in(own, 4), (amount // 2,), 0, 1 << 20) % (room + 1)
    lengths = lengths.at[source_of].add(-moved).at[taker].add(moved)
    members = jnp.searchsorted(jnp.cumsum(lengths), jnp.arange(rows * top), side="right").astype(jnp.int32)
    listing = members.reshape(top, rows).T
    listing = listing[jax.random.permutation(jax.random.fold_in(own, 1), rows)]
    rotation = jax.random.randint(jax.random.fold_in(own, 2), (rows, 1), 0, top)
    return jnp.take_along_axis(listing, (jnp.arange(top)[None, :] + rotation) % top, axis=1)


def shares(count, total, limit, lean, full):
    weights = [(1 << 20) // math.isqrt(rank ** lean) + 1 for rank in range(1, count + 1)]
    largest = limit if full else min(limit, max(-(-total // count), total * weights[0] // sum(weights)))
    least = 1 if total - largest >= count - 1 else 0
    given, surplus = [largest] + [least] * (count - 1), total - largest - least * (count - 1)
    while surplus > 0:
        free = [i for i in range(1, count) if given[i] < largest] or [i for i in range(1, count) if given[i] < limit]
        pool, remaining = sum([weights[i] for i in free]), surplus
        for i in free:
            extra = min(limit - given[i], max(1, remaining * weights[i] // pool), surplus)
            given[i] = given[i] + extra
            surplus = surplus - extra
    return np.array(given)


def noise(rng, extent, scale, bound, cuts=(), kind=jnp.bfloat16):
    values = scale * jax.random.normal(rng, extent, jnp.float32)
    if cuts:
        values = values * level_of(rng, extent, cuts, -0.22, 0.18)
    return jnp.clip(values, -bound, bound).astype(kind)


def setup_inputs(seed: int = 0) -> dict:
    key_of = jax.random.split(jax.random.key(seed), 7)
    out_grad = draw_out_grad(jax.random.fold_in(key_of[6], 71), 0)
    routes_keys = jax.random.split(jax.random.fold_in(key_of[1], 1), TOKENS // TOK_DEV)
    routes_turns = jax.random.permutation(jax.random.fold_in(key_of[1], 3), TOKENS // TOK_DEV)
    routes = jax.vmap(lambda own, number: routed_block(jax.random.fold_in(key_of[1], 2), own, number, TOK_DEV, EXPERTS, 1, SLOT, 2))(routes_keys, routes_turns).reshape((TOKENS, 1))
    pre_act = draw_pre_act(jax.random.fold_in(key_of[6], 71), 0)
    out_weight = noise(key_of[3], (EXPERTS, FF, D), FF ** -0.5, 0.109375, ((0, 16), (1, 2)))
    row_factor = jnp.clip(jnp.exp(math.log(100.0) - 4.6051702 * jax.random.uniform(key_of[4], (EXPERTS, FF), jnp.float32) ** level_of(key_of[4], (EXPERTS, FF), ((0, 16), (1, 2)), -0.2, 0.2)), 1.0, 100.0)
    col_factor = jnp.clip(jnp.exp(math.log(100.0) - 4.6051702 * jax.random.uniform(key_of[5], (EXPERTS, D), jnp.float32) ** level_of(key_of[5], (EXPERTS, D), ((0, 16),), -0.2, 0.2)), 1.0, 100.0)
    return {"out_grad": out_grad, "routes": routes, "pre_act": pre_act, "out_weight": out_weight, "row_factor": row_factor, "col_factor": col_factor}


def slot_of(routes):
    blocks = routes.reshape(N_DP * N_EXPERT, TOK_DEV)
    same = blocks[:, :, None] == blocks[:, None, :]
    earlier = jnp.arange(TOK_DEV)[None, :] < jnp.arange(TOK_DEV)[:, None]
    order_in = lax.optimization_barrier(jnp.sum((same & earlier[None]).astype(jnp.int32), axis=2)).astype(jnp.int32)
    return (blocks * SLOT + order_in).astype(jnp.int32)

def expert_step(items):
    dy_rows, pre_rows, weight, row_old, col_old = items
    weight_f = weight.astype(jnp.float32)
    back_f = jnp.dot(dy_rows.astype(jnp.float32), weight_f.T)
    back = jnp.where(pre_rows > 0, back_f, 0.0).astype(jnp.bfloat16)
    hidden = jnp.maximum(pre_rows, 0).astype(jnp.float32)
    gradient = jnp.dot(hidden.T, dy_rows.astype(jnp.float32))
    squares = gradient * gradient + 1e-30
    row_new = 0.8 * row_old + 0.2 * lax.optimization_barrier(jnp.mean(squares, axis=1))
    col_new = 0.8 * col_old + 0.2 * lax.optimization_barrier(jnp.mean(squares, axis=0))
    second = row_new[:, None] * col_new[None, :]
    update = gradient * lax.rsqrt(second)
    spread = jnp.sqrt(jnp.mean(update * update))
    update = update / jnp.maximum(1.0, spread / 0.01)
    weight_new = (weight_f - update).astype(jnp.bfloat16)
    return (back, weight_new, row_new, col_new)

def reference(out_grad, routes, pre_act, out_weight, row_factor, col_factor):
    blocks = N_DP * N_EXPERT
    slots = slot_of(routes)
    dy_blocks = out_grad.reshape(blocks, TOK_DEV, D)
    outgoing = jnp.zeros((blocks, R, D), jnp.bfloat16)
    outgoing = outgoing.at[jnp.arange(blocks)[:, None], slots].set(dy_blocks)
    arrived = outgoing.reshape(N_DP, N_EXPERT, N_EXPERT, SLOT, D).transpose(2, 0, 1, 3, 4)
    arrived = arrived.reshape(N_EXPERT, N_DP * R, D)
    pre_rows = pre_act.reshape(N_DP, N_EXPERT, R, FF).transpose(1, 0, 2, 3).reshape(N_EXPERT, N_DP * R, FF)
    back, weight_new, row_new, col_new = lax.map(expert_step, (arrived, pre_rows, out_weight, row_factor, col_factor))
    returned = back.reshape(N_EXPERT, N_DP, N_EXPERT, SLOT, FF).transpose(1, 2, 0, 3, 4).reshape(blocks, R, FF)
    hidden_grad = jnp.take_along_axis(returned, slots[:, :, None], axis=1)
    return (hidden_grad.reshape(TOKENS, FF), weight_new, row_new, col_new)
```

```python
import functools
import jax
import jax.numpy as jnp
from jax import lax
from jax.experimental import pallas as pl
from jax.experimental.pallas import tpu as pltpu
from jax.sharding import PartitionSpec as P

MESH = pl.DeviceIdType.MESH
F32, BF16 = jnp.float32, jnp.bfloat16


def up128(n):
    return -(-n // 128) * 128


def dot(a, b, ca=1, cb=0):
    return lax.dot_general(a, b, (((ca,), (cb,)), ((), ())), preferred_element_type=F32)


def onehot(hit):
    return jnp.where(hit, 1.0, 0.0).astype(BF16)


def kernel(cfg, og_h, rrow_h, pre, w, rf_h, cf_h,
           hid, neww, newrow, newcol,
           og, rrow, rf, cf, qn, qt,
           dy_out, dy_all, dyn, pre_all, wv, grad, snd, ret, colst, place, colacc, cspad, cscol,
           loc, flood, dy_s, dy_r, fw_s, fw_r, pre_s, pre_r, rt_s, rt_r, st_s, st_r):
    n_dp, n_e, slot, chunk, deep = cfg
    d, tok = og.shape
    ff = wv.shape[1]
    packed = slot > 8
    half, dp_off, h0 = ff // 2, up128(d), d // 2 // 128 * 128
    rest = d - 2 * h0
    bits = n_e.bit_length() - 1
    g = n_e // 4
    n = g * slot
    i, e = lax.axis_index("dp"), lax.axis_index("expert")
    others = [(o, lax.rem(i + o, n_dp)) for o in range(1, n_dp)]

    def flip(x, b):
        return x + (1 - 2 * lax.rem(lax.div(x, 1 << b), 2)) * (1 << b)

    def loop(count, act):
        def step(k, _):
            act(k)
            return 0
        lax.fori_loop(0, count, step, 0)

    barrier = pltpu.get_barrier_semaphore()
    for _, t in others:
        pl.semaphore_signal(barrier, inc=1, device_id=(t, e), device_id_type=MESH)
    for b in range(bits):
        pl.semaphore_signal(barrier, inc=1, device_id=(i, flip(e, b)), device_id_type=MESH)

    cols = lambda t: pl.ds(pl.multiple_of(t * ff, 128), ff)
    loads = [pltpu.make_async_copy(x, y, loc.at[k]) for k, (x, y) in enumerate((
        (rrow_h, rrow), (og_h, og), (w.at[0], wv), (pre.at[:, cols(i)], pre_all.at[i]), (rf_h, rf),
        (cf_h, cf)))]
    for load in loads:
        load.start()

    def tables(q, rows, cells, axis):
        for k in range(q.shape[0]):
            row = lax.broadcasted_iota(jnp.int32, (rows, cells), axis)
            cell = lax.broadcasted_iota(jnp.int32, (rows, cells), 1 - axis)
            at = cell & 7
            wants = slot * (cell >> 3) + at + (0, 8, 4)[k]
            held = (at < min(slot, 8), at < slot - 8, at >= 4)[k]
            q[k] = onehot((row == wants) & held)

    tables(qn, n, g * 8, 0)
    tables(qt, g * 8, n, 1)

    loads[0].wait()
    named = jnp.broadcast_to(rrow[...].astype(F32), (tok, tok))
    same = named == named.T
    at_row = lax.broadcasted_iota(jnp.int32, (tok, tok), 0)
    at_col = lax.broadcasted_iota(jnp.int32, (tok, tok), 1)
    order = jnp.sum(jnp.where(same & (at_row < at_col), 1.0, 0.0), axis=0, keepdims=True)
    base = rrow[...].astype(F32) * 8.0 + order
    rows = lax.broadcasted_iota(jnp.int32, (n_e * 8, tok), 0).astype(F32)
    place[0] = onehot(rows == jnp.where(order < 8.0, base, -1.0))
    if packed:
        place[1] = onehot(rows == jnp.where(order >= 8.0, base - 8.0, -1.0))
        place[2] = onehot(rows == jnp.where(order >= 8.0, base - 4.0, -1.0))
    loads[1].wait()
    dy_out[:, :, 0:d] = dot(place[0], og[...], 1, 1).reshape(n_e, 8, d).astype(BF16)
    if packed:
        tail = dot(place[1], og[0:h0, :], 1, 1) + dot(place[2], og[h0:2 * h0, :], 1, 1)
        dy_out[:, :, dp_off:dp_off + h0] = tail.reshape(n_e, 8, h0).astype(BF16)
        if rest:
            more = dot(place[1], og[2 * h0:d, :], 1, 1)
            dy_out[:, :, d:d + rest] = more.reshape(n_e, 8, rest).astype(BF16)

    quarter = lax.div(e, g)
    order_k = (2, 3, 1, 0)
    group = {0: quarter, 1: flip(quarter, 0), 2: flip(quarter, 1), 3: flip(flip(quarter, 0), 1)}

    def members(k, act):
        if k:
            loop(g, lambda m: act(group[k] * g + m))
        else:
            loop(g - 1, lambda m: act(quarter * g + lax.rem(e + 1 + m, g)))

    def send_dy(k, t):
        return pltpu.make_async_remote_copy(
            src_ref=dy_out.at[t], dst_ref=dy_all.at[i, e], send_sem=dy_s.at[0],
            recv_sem=dy_r.at[k], device_id=(i, t), device_id_type=MESH)

    def send_pre(o, t):
        return pltpu.make_async_remote_copy(
            src_ref=pre.at[:, cols(t)], dst_ref=pre_all.at[i], send_sem=pre_s.at[o - 1],
            recv_sem=pre_r.at[n_dp - o - 1], device_id=(t, e), device_id_type=MESH)

    def send_fw(o, t, k):
        part = pl.ds(group[k] * g, g)
        return pltpu.make_async_remote_copy(
            src_ref=dy_all.at[i, part], dst_ref=dy_all.at[i, part], send_sem=fw_s.at[o - 1],
            recv_sem=fw_r.at[n_dp - o - 1, k], device_id=(t, e), device_id_type=MESH)

    def send_ret(o, t, j):
        return pltpu.make_async_remote_copy(
            src_ref=snd.at[t, j], dst_ref=ret.at[i, e], send_sem=rt_s.at[o],
            recv_sem=rt_r.at[lax.rem(n_dp - o, n_dp)], device_id=(t, j), device_id_type=MESH)

    def send_st(o, t):
        return pltpu.make_async_remote_copy(
            src_ref=colst.at[i], dst_ref=colst.at[i], send_sem=st_s.at[o - 1],
            recv_sem=st_r.at[n_dp - o - 1], device_id=(t, e), device_id_type=MESH)

    def meet(b):
        pl.semaphore_signal(flood.at[b], inc=1, device_id=(i, flip(e, b)), device_id_type=MESH)
        pl.semaphore_wait(flood.at[b], 1)

    with jax.named_scope("bar"):
        pl.semaphore_wait(barrier, bits + n_dp - 1)
    for o, t in others:
        send_pre(o, t).start()
    with jax.named_scope("flood"):
        for b in range(bits - 2):
            meet(b)
    members(2, lambda t: send_dy(2, t).start())
    with jax.named_scope("flood2"):
        meet(bits - 2)
    for k in (3, 1, 0):
        members(k, lambda t: send_dy(k, t).start())
    own = pltpu.make_async_copy(dy_out.at[e], dy_all.at[i, e], dy_r.at[0])
    own.start()

    colacc[...] = jnp.zeros_like(colacc)

    def flat_rows(x):
        return x.astype(F32).reshape(x.shape[0] * 8, x.shape[2]).astype(BF16)

    def back(t, k):
        part = pl.ds(group[k] * g, g)
        where = pl.ds(pl.multiple_of(group[k] * n, 16), n)
        dy = dot(qn[0], flat_rows(dy_all[t, part, :, 0:d]))
        if packed:
            q_lo, q_hi = qn[1], qn[2]
            tail = flat_rows(dy_all[t, part, :, dp_off:dp_off + h0])
            pieces = [dot(q_lo, tail), dot(q_hi, tail)]
            if rest:
                ends = dot(q_lo, flat_rows(dy_all[t, part, :, 2 * h0:dp_off]))
                pieces.append(ends[:, d - 2 * h0:d - 2 * h0 + rest])
            dy = dy + jnp.concatenate(pieces, axis=1)
        dy = dy.astype(BF16)
        dyn[t, where, :] = dy
        tail = None
        for c in range(2 if packed else 1):
            wide = half if packed else ff
            span = slice(c * wide, c * wide + wide)
            bk = dot(dy, wv[:, span])
            keep = pre_all[t, where, span].astype(F32) > 0.0
            bk = jnp.where(keep, bk, 0.0).astype(BF16)
            snd[t, part, :, span] = dot(qt[0], bk).reshape(g, 8, wide).astype(BF16)
            if packed:
                more = dot(qt[1 + c], bk)
                tail = more if tail is None else tail + more
        if packed:
            snd[t, part, :, ff:ff + half] = tail.reshape(g, 8, half).astype(BF16)

    for k in order_k:
        part = pl.ds(group[k] * g, g)
        with jax.named_scope("recv%d" % k):
            pltpu.make_async_copy(dy_all.at[0, part], dy_all.at[i, part], dy_r.at[k]).wait()
        for o, t in others:
            send_fw(o, t, k).start()
        if k == order_k[0]:
            with jax.named_scope("waitw"):
                loads[2].wait()
                loads[3].wait()
        with jax.named_scope("back%d" % k):
            back(i, k)
        members(k, lambda j: send_ret(0, i, j).start())
    own_ret = pltpu.make_async_copy(snd.at[i, e], ret.at[i, e], rt_r.at[0])
    own_ret.start()

    for o, t in others:
        with jax.named_scope("waitpre"):
            pltpu.make_async_copy(pre_all.at[i], pre_all.at[t], pre_r.at[o - 1]).wait()
        for k in order_k:
            part = pl.ds(group[k] * g, g)
            with jax.named_scope("waitfw%d" % k):
                pltpu.make_async_copy(dy_all.at[i, part], dy_all.at[t, part], fw_r.at[o - 1, k]).wait()
            with jax.named_scope("backx%d" % k):
                back(t, k)
            loop(g, lambda m: send_ret(o, t, group[k] * g + m).start())

    loads[4].wait()
    loads[5].wait()

    def gradient(c):
        span = pl.ds(pl.multiple_of(c * chunk, 128), chunk)
        acc = None
        for t in range(n_dp):
            part = dot(dyn[t], jnp.maximum(pre_all[t, :, span], 0), 0, 0)
            acc = part if acc is None else acc + part
        grad[:, span] = acc
        sq = acc * acc
        rn = 0.8 * rf[0:1, span] + 0.2 * (jnp.sum(sq, axis=0, keepdims=True) / d + 1e-30)
        newrow[0:1, span] = rn
        for k, x in enumerate((sq, sq * (1.0 / rn))):
            folded = x[:, 0:128]
            for b in range(1, chunk // 128):
                folded = folded + x[:, b * 128:b * 128 + 128]
            colacc[k, 0:d, :] += folded

    with jax.named_scope("grad"):
        loop(ff // chunk, gradient)
    blocks = [(b, min(b + 128, d)) for b in range(0, d, 128)]
    for k in range(2):
        for lo, hi in blocks:
            sums = jnp.sum(colacc[k, lo:lo + 128, :].T, axis=0, keepdims=True)
            colst[i, k:k + 1, lo:hi] = sums[:, 0:hi - lo]
    for o, t in others:
        send_st(o, t).start()

    def deliver(o, t):
        with jax.named_scope("waitret%d" % o):
            pltpu.make_async_copy(snd.at[0], ret.at[t], rt_r.at[o]).wait()
        with jax.named_scope("hid%d" % o):
            for c in range(2 if packed else 1):
                wide = half if packed else ff
                got = dot(place[0], flat_rows(ret[t, :, :, c * wide:c * wide + wide]), 0, 0)
                if packed:
                    got = got + dot(place[1 + c], flat_rows(ret[t, :, :, ff:ff + half]), 0, 0)
                hid[:, pl.ds(pl.multiple_of(t * ff + c * wide, 128), wide)] = got.astype(BF16)

    deliver(0, i)
    with jax.named_scope("waitst"):
        for o, t in others:
            pltpu.make_async_copy(colst.at[i], colst.at[t], st_r.at[o - 1]).wait()
    col, weighted = jnp.zeros((1, d), F32), jnp.zeros((1, d), F32)
    for t in range(n_dp):
        col = col + colst[t, 0:1, :]
        weighted = weighted + colst[t, 1:2, :]
    full = ff * n_dp
    cn = 0.8 * cf[...] + 0.2 * (col / full + 1e-30)
    newcol[...] = cn
    spread = jnp.sqrt(jnp.sum(weighted / cn, axis=1, keepdims=True) / (full * d))
    cspad[...] = jnp.zeros_like(cspad)
    cspad[0:1, 0:d] = lax.rsqrt(cn) / jnp.maximum(1.0, spread / 0.01)
    for lo, hi in blocks:
        cscol[lo:lo + 128, :] = jnp.broadcast_to(cspad[0:1, lo:lo + 128], (128, 128)).T

    def apply(c):
        span = pl.ds(pl.multiple_of(c * deep, 16), deep)
        update = grad[span, :] * lax.rsqrt(newrow[...]) * cscol[span, 0:1]
        neww[0, span, :] = (wv[span, :].astype(F32) - update).astype(BF16)

    with jax.named_scope("apply"):
        loop(d // deep, apply)

    for o, t in others:
        deliver(o, t)

    def sent(src, sem):
        pltpu.make_async_copy(src, src, sem).wait()

    with jax.named_scope("sent"):
        sent(dy_out.at[0:n_e - 1], dy_s.at[0])
        sent(snd.at[0, 0:n_e - 1], rt_s.at[0])
        for o, t in others:
            sent(pre_all.at[0], pre_s.at[o - 1])
            sent(dy_all.at[0], fw_s.at[o - 1])
            sent(snd.at[0], rt_s.at[o])
            sent(colst.at[0], st_s.at[o - 1])


def flush(a, b, c, d, ao, bo, co, do, sem):
    pairs = ((b, bo), (a, ao), (c, co), (d, do))
    copies = [pltpu.make_async_copy(x, y, sem.at[k]) for k, (x, y) in enumerate(pairs)]
    for copy in copies:
        copy.start()
    for copy in copies:
        copy.wait()


def shards(out_grad, routes, pre_act, out_weight, row_factor, col_factor):
    n_dp, n_e = lax.axis_size("dp"), lax.axis_size("expert")
    tok, d = out_grad.shape
    r = pre_act.shape[0]
    ff = out_weight.shape[1]
    slot = r // n_e
    packed = slot > 8
    assert slot <= 12
    kinds = 3 if packed else 1
    assert n_e >= 4 and n_e & (n_e - 1) == 0
    g = n_e // 4
    chunk = next(c for c in (384, 256, 128) if ff % c == 0)
    deep = max(c for c in range(16, 257, 16) if d % c == 0)
    wide_d = up128(d) + d // 2 // 128 * 128 if packed else d
    assert not packed or 2 * d - d // 256 * 256 <= up128(d)
    wide_f = ff + ff // 2 if packed else ff
    vm = pl.BlockSpec(memory_space=pltpu.VMEM)
    hbm = pl.BlockSpec(memory_space=pl.ANY)
    dma = pltpu.SemaphoreType.DMA
    out = pltpu.VMEM
    hid, neww, newrow, newcol = pl.pallas_call(
        functools.partial(kernel, (n_dp, n_e, slot, chunk, deep)),
        out_shape=(out((tok, ff * n_dp), BF16), out((1, d, ff), BF16),
                   out((1, ff), F32), out((1, d), F32)),
        in_specs=[hbm] * 6,
        out_specs=(vm, vm, vm, vm),
        scratch_shapes=[
            pltpu.VMEM((d, tok), BF16),
            pltpu.VMEM((1, tok), jnp.int32),
            pltpu.VMEM((1, ff), F32),
            pltpu.VMEM((1, d), F32),
            pltpu.VMEM((kinds, g * slot, g * 8), BF16),
            pltpu.VMEM((kinds, g * 8, g * slot), BF16),
            pltpu.VMEM((n_e, 8, wide_d), BF16),
            pltpu.VMEM((n_dp, n_e, 8, wide_d), BF16),
            pltpu.VMEM((n_dp, r, d), BF16),
            pltpu.VMEM((n_dp, r, ff), BF16),
            pltpu.VMEM((d, ff), BF16),
            pltpu.VMEM((d, ff), F32),
            pltpu.VMEM((n_dp, n_e, 8, wide_f), BF16),
            pltpu.VMEM((n_dp, n_e, 8, wide_f), BF16),
            pltpu.VMEM((n_dp, 2, d), F32),
            pltpu.VMEM((kinds, n_e * 8, tok), BF16),
            pltpu.VMEM((2, up128(d), 128), F32),
            pltpu.VMEM((1, up128(d)), F32),
            pltpu.VMEM((up128(d), 128), F32),
            dma((6,)), pltpu.SemaphoreType.REGULAR((n_e.bit_length() - 2,)), dma((1,)), dma((4,)),
            dma((n_dp - 1,)), dma((n_dp - 1, 4)), dma((n_dp - 1,)), dma((n_dp - 1,)),
            dma((n_dp,)), dma((n_dp,)), dma((n_dp - 1,)), dma((n_dp - 1,)),
        ],
        compiler_params=pltpu.CompilerParams(
            collective_id=0, has_side_effects=True, vmem_limit_bytes=59 * 1024 * 1024),
    )(out_grad.T, routes.reshape(1, tok), pre_act, jnp.swapaxes(out_weight, 1, 2), row_factor,
      col_factor)
    held = (hid, neww, newrow, newcol)
    hid, neww, newrow, newcol = pl.pallas_call(
        flush,
        out_shape=tuple(jax.ShapeDtypeStruct(x.shape, x.dtype) for x in held),
        in_specs=[vm] * 4,
        out_specs=[hbm] * 4,
        scratch_shapes=[dma((4,))],
        compiler_params=pltpu.CompilerParams(vmem_limit_bytes=1024 * 1024),
    )(*held)
    return hid, jnp.swapaxes(neww, 1, 2), newrow, newcol


def solution(mesh):
    placed = (
        P(("dp", "expert"), None),
        P(("dp", "expert"), None),
        P(("dp", "expert"), None),
        P("expert", "dp", None),
        P("expert", "dp"),
        P("expert", None),
    )
    return jax.shard_map(
        shards,
        mesh=mesh,
        in_specs=placed,
        out_specs=(
            P(("dp", "expert"), None),
            P("expert", "dp", None),
            P("expert", "dp"),
            P("expert", None),
        ),
        check_vma=False,
    )
```

```python
import functools
import jax
import jax.numpy as jnp
from jax import lax
from jax.experimental import pallas as pl
from jax.experimental.pallas import tpu as pltpu
from jax.sharding import PartitionSpec as P

MESH = pl.DeviceIdType.MESH
F32, BF16 = jnp.float32, jnp.bfloat16


def up128(n):
    return -(-n // 128) * 128


def dot(a, b, ca=1, cb=0):
    return lax.dot_general(a, b, (((ca,), (cb,)), ((), ())), preferred_element_type=F32)


def onehot(hit):
    return jnp.where(hit, 1.0, 0.0).astype(BF16)


def flat_rows(x):
    return x.astype(F32).reshape(x.shape[0] * 8, x.shape[2]).astype(BF16)


def kernel(cfg, og_h, rrow_h, pre, w, rf_h, cf_h,
           ret, place, neww, newrow, newcol,
           og, rrow, rf, cf, qn, qt,
           dy_out, dy_all, dyn, pre_all, wv, grad, snd, colst, colacc, cspad, cscol,
           loc, flood, dy_s, dy_r, fw_s, fw_r, pre_s, pre_r, rt_s, rt_r, st_s, st_r):
    n_dp, n_e, slot, chunk, deep = cfg
    d, tok = og.shape
    ff = wv.shape[1]
    packed = slot > 8
    half, dp_off, h0 = ff // 2, up128(d), d // 2 // 128 * 128
    rest = d - 2 * h0
    bits = n_e.bit_length() - 1
    g = n_e // 4
    n = g * slot
    i, e = lax.axis_index("dp"), lax.axis_index("expert")
    others = [(o, lax.rem(i + o, n_dp)) for o in range(1, n_dp)]

    def flip(x, b):
        return x + (1 - 2 * lax.rem(lax.div(x, 1 << b), 2)) * (1 << b)

    def loop(count, act):
        def step(k, _):
            act(k)
            return 0
        lax.fori_loop(0, count, step, 0)

    barrier = pltpu.get_barrier_semaphore()
    for _, t in others:
        pl.semaphore_signal(barrier, inc=1, device_id=(t, e), device_id_type=MESH)
    for b in range(bits):
        pl.semaphore_signal(barrier, inc=1, device_id=(i, flip(e, b)), device_id_type=MESH)

    cols = lambda t: pl.ds(pl.multiple_of(t * ff, 128), ff)
    loads = [pltpu.make_async_copy(x, y, loc.at[k]) for k, (x, y) in enumerate((
        (rrow_h, rrow), (og_h, og), (w.at[0], wv), (pre.at[:, cols(i)], pre_all.at[i]), (rf_h, rf),
        (cf_h, cf)))]
    for load in loads:
        load.start()

    def tables(q, rows, cells, axis):
        for k in range(q.shape[0]):
            row = lax.broadcasted_iota(jnp.int32, (rows, cells), axis)
            cell = lax.broadcasted_iota(jnp.int32, (rows, cells), 1 - axis)
            at = cell & 7
            wants = slot * (cell >> 3) + at + (0, 8, 4)[k]
            held = (at < min(slot, 8), at < slot - 8, at >= 4)[k]
            q[k] = onehot((row == wants) & held)

    tables(qn, n, g * 8, 0)
    tables(qt, g * 8, n, 1)

    loads[0].wait()
    named = jnp.broadcast_to(rrow[...].astype(F32), (tok, tok))
    same = named == named.T
    at_row = lax.broadcasted_iota(jnp.int32, (tok, tok), 0)
    at_col = lax.broadcasted_iota(jnp.int32, (tok, tok), 1)
    order = jnp.sum(jnp.where(same & (at_row < at_col), 1.0, 0.0), axis=0, keepdims=True)
    base = rrow[...].astype(F32) * 8.0 + order
    rows = lax.broadcasted_iota(jnp.int32, (n_e * 8, tok), 0).astype(F32)
    place[0] = onehot(rows == jnp.where(order < 8.0, base, -1.0))
    if packed:
        place[1] = onehot(rows == jnp.where(order >= 8.0, base - 8.0, -1.0))
        place[2] = onehot(rows == jnp.where(order >= 8.0, base - 4.0, -1.0))
    loads[1].wait()
    dy_out[:, :, 0:d] = dot(place[0], og[...], 1, 1).reshape(n_e, 8, d).astype(BF16)
    if packed:
        tail = dot(place[1], og[0:h0, :], 1, 1) + dot(place[2], og[h0:2 * h0, :], 1, 1)
        dy_out[:, :, dp_off:dp_off + h0] = tail.reshape(n_e, 8, h0).astype(BF16)
        if rest:
            more = dot(place[1], og[2 * h0:d, :], 1, 1)
            dy_out[:, :, d:d + rest] = more.reshape(n_e, 8, rest).astype(BF16)

    quarter = lax.div(e, g)
    group = {0: quarter, 1: flip(quarter, 0), 2: flip(quarter, 1), 3: flip(flip(quarter, 0), 1)}

    def members(k, act):
        if k:
            loop(g, lambda m: act(group[k] * g + m))
        else:
            loop(g - 1, lambda m: act(quarter * g + lax.rem(e + 1 + m, g)))

    def send_dy(k, t):
        return pltpu.make_async_remote_copy(
            src_ref=dy_out.at[t], dst_ref=dy_all.at[i, e], send_sem=dy_s.at[0],
            recv_sem=dy_r.at[k], device_id=(i, t), device_id_type=MESH)

    def rows_of(k):
        return pl.ds(pl.multiple_of(group[k] * n, 16), n)

    def send_pre(o, t, k):
        return pltpu.make_async_remote_copy(
            src_ref=pre.at[rows_of(k), cols(t)], dst_ref=pre_all.at[i, rows_of(k)],
            send_sem=pre_s.at[o - 1], recv_sem=pre_r.at[n_dp - o - 1, k], device_id=(t, e),
            device_id_type=MESH)

    def send_fw(o, t, k):
        part = pl.ds(group[k] * g, g)
        return pltpu.make_async_remote_copy(
            src_ref=dy_all.at[i, part], dst_ref=dy_all.at[i, part], send_sem=fw_s.at[o - 1],
            recv_sem=fw_r.at[n_dp - o - 1, k], device_id=(t, e), device_id_type=MESH)

    def send_ret(o, t, j):
        return pltpu.make_async_remote_copy(
            src_ref=snd.at[t, j], dst_ref=ret.at[i, e], send_sem=rt_s.at[o],
            recv_sem=rt_r.at[lax.rem(n_dp - o, n_dp)], device_id=(t, j), device_id_type=MESH)

    def send_st(o, t):
        return pltpu.make_async_remote_copy(
            src_ref=colst.at[i], dst_ref=colst.at[i], send_sem=st_s.at[o - 1],
            recv_sem=st_r.at[n_dp - o - 1], device_id=(t, e), device_id_type=MESH)

    def meet(b):
        pl.semaphore_signal(flood.at[b], inc=1, device_id=(i, flip(e, b)), device_id_type=MESH)
        pl.semaphore_wait(flood.at[b], 1)

    with jax.named_scope("bar"):
        pl.semaphore_wait(barrier, bits + n_dp - 1)
    for k in (2, 3, 1):
        for o, t in others:
            send_pre(o, t, k).start()
    across = flip(e, bits - 1)
    send_dy(2, across).start()
    with jax.named_scope("flood"):
        for b in range(bits - 2):
            meet(b)
            first = lax.div(flip(across, b), 1 << b) * (1 << b)
            loop(1 << b, lambda m: send_dy(2, first + m).start())
    with jax.named_scope("flood2"):
        meet(bits - 2)
    for k in (3, 1, 0):
        members(k, lambda t: send_dy(k, t).start())
    own = pltpu.make_async_copy(dy_out.at[e], dy_all.at[i, e], dy_r.at[0])
    own.start()

    colacc[...] = jnp.zeros_like(colacc)

    def back(t, k):
        part = pl.ds(group[k] * g, g)
        where = rows_of(k)
        dy = dot(qn[0], flat_rows(dy_all[t, part, :, 0:d]))
        if packed:
            q_lo, q_hi = qn[1], qn[2]
            tail = flat_rows(dy_all[t, part, :, dp_off:dp_off + h0])
            pieces = [dot(q_lo, tail), dot(q_hi, tail)]
            if rest:
                ends = dot(q_lo, flat_rows(dy_all[t, part, :, 2 * h0:dp_off]))
                pieces.append(ends[:, d - 2 * h0:d - 2 * h0 + rest])
            dy = dy + jnp.concatenate(pieces, axis=1)
        dy = dy.astype(BF16)
        dyn[t, where, :] = dy
        tail = None
        for c in range(2 if packed else 1):
            wide = half if packed else ff
            span = slice(c * wide, c * wide + wide)
            bk = dot(dy, wv[:, span])
            keep = pre_all[t, where, span].astype(F32) > 0.0
            bk = jnp.where(keep, bk, 0.0).astype(BF16)
            snd[t, part, :, span] = dot(qt[0], bk).reshape(g, 8, wide).astype(BF16)
            if packed:
                more = dot(qt[1 + c], bk)
                tail = more if tail is None else tail + more
        if packed:
            snd[t, part, :, ff:ff + half] = tail.reshape(g, 8, half).astype(BF16)

    def arrive(k):
        part = pl.ds(group[k] * g, g)
        with jax.named_scope("recv%d" % k):
            pltpu.make_async_copy(dy_all.at[0, part], dy_all.at[i, part], dy_r.at[k]).wait()

    def forward(k):
        for o, t in others:
            send_fw(o, t, k).start()

    def near(k):
        with jax.named_scope("back%d" % k):
            back(i, k)
        members(k, lambda j: send_ret(0, i, j).start())

    def await_cross(k):
        part = pl.ds(group[k] * g, g)
        for o, t in others:
            with jax.named_scope("waitpre%d" % k):
                pltpu.make_async_copy(
                    pre_all.at[i, rows_of(k)], pre_all.at[t, rows_of(k)], pre_r.at[o - 1, k]).wait()
            with jax.named_scope("waitfw%d" % k):
                pltpu.make_async_copy(dy_all.at[i, part], dy_all.at[t, part], fw_r.at[o - 1, k]).wait()

    def back_cross(k):
        for _, t in others:
            with jax.named_scope("backx%d" % k):
                back(t, k)

    def cross(k):
        await_cross(k)
        back_cross(k)

    def send_cross(k):
        for o, t in others:
            loop(g, lambda m: send_ret(o, t, group[k] * g + m).start())

    arrive(2)
    forward(2)
    loads[2].wait()
    loads[3].wait()
    near(2)
    arrive(3)
    forward(3)
    for o, t in others:
        send_pre(o, t, 0).start()
    near(3)
    arrive(1)
    forward(1)
    near(1)
    arrive(0)
    forward(0)
    near(0)
    own_ret = pltpu.make_async_copy(snd.at[i, e], ret.at[i, e], rt_r.at[0])
    own_ret.start()
    cross(2)
    cross(3)
    cross(1)
    send_cross(2)
    send_cross(3)
    await_cross(0)
    send_cross(1)
    back_cross(0)

    loads[4].wait()
    loads[5].wait()

    def gradient(c):
        span = pl.ds(pl.multiple_of(c * chunk, 128), chunk)
        acc = None
        for t in range(n_dp):
            part = dot(dyn[t], jnp.maximum(pre_all[t, :, span], 0), 0, 0)
            acc = part if acc is None else acc + part
        grad[:, span] = acc
        sq = acc * acc
        rn = 0.8 * rf[0:1, span] + 0.2 * (jnp.sum(sq, axis=0, keepdims=True) / d + 1e-30)
        newrow[0:1, span] = rn
        for k, x in enumerate((sq, sq * (1.0 / rn))):
            folded = x[:, 0:128]
            for b in range(1, chunk // 128):
                folded = folded + x[:, b * 128:b * 128 + 128]
            colacc[k, 0:d, :] += folded

    with jax.named_scope("grad"):
        loop(ff // chunk, gradient)
    blocks = [(b, min(b + 128, d)) for b in range(0, d, 128)]
    for k in range(2):
        for lo, hi in blocks:
            sums = jnp.sum(colacc[k, lo:lo + 128, :].T, axis=0, keepdims=True)
            colst[i, k:k + 1, lo:hi] = sums[:, 0:hi - lo]
    for o, t in others:
        send_st(o, t).start()
    send_cross(0)

    with jax.named_scope("waitst"):
        for o, t in others:
            pltpu.make_async_copy(colst.at[i], colst.at[t], st_r.at[o - 1]).wait()
    col, weighted = jnp.zeros((1, d), F32), jnp.zeros((1, d), F32)
    for t in range(n_dp):
        col = col + colst[t, 0:1, :]
        weighted = weighted + colst[t, 1:2, :]
    full = ff * n_dp
    cn = 0.8 * cf[...] + 0.2 * (col / full + 1e-30)
    newcol[...] = cn
    spread = jnp.sqrt(jnp.sum(weighted / cn, axis=1, keepdims=True) / (full * d))
    cspad[...] = jnp.zeros_like(cspad)
    cspad[0:1, 0:d] = lax.rsqrt(cn) / jnp.maximum(1.0, spread / 0.01)
    for lo, hi in blocks:
        cscol[lo:lo + 128, :] = jnp.broadcast_to(cspad[0:1, lo:lo + 128], (128, 128)).T

    def apply(c):
        span = pl.ds(pl.multiple_of(c * deep, 16), deep)
        update = grad[span, :] * lax.rsqrt(newrow[...]) * cscol[span, 0:1]
        neww[0, span, :] = (wv[span, :].astype(F32) - update).astype(BF16)

    with jax.named_scope("apply"):
        loop(d // deep, apply)

    for o, t in [(0, i)] + others:
        with jax.named_scope("waitret%d" % o):
            pltpu.make_async_copy(snd.at[0], ret.at[t], rt_r.at[o]).wait()

    def sent(src, sem):
        pltpu.make_async_copy(src, src, sem).wait()

    with jax.named_scope("sent"):
        sent(dy_out.at[0:n_e - 1], dy_s.at[0])
        sent(snd.at[0, 0:n_e - 1], rt_s.at[0])
        for o, t in others:
            sent(pre_all.at[0], pre_s.at[o - 1])
            sent(dy_all.at[0], fw_s.at[o - 1])
            sent(snd.at[0], rt_s.at[o])
            sent(colst.at[0], st_s.at[o - 1])


def finish(packed, ff, ret, place, neww, newrow, newcol, hid_o, neww_o, newrow_o, newcol_o, hid, sem):
    copies = [pltpu.make_async_copy(x, y, sem.at[k]) for k, (x, y) in enumerate((
        (neww, neww_o), (newrow, newrow_o), (newcol, newcol_o)))]
    for copy in copies:
        copy.start()
    half = ff // 2
    wide = half if packed else ff
    for t in range(ret.shape[0]):
        for c in range(2 if packed else 1):
            got = dot(place[0], flat_rows(ret[t, :, :, c * wide:c * wide + wide]), 0, 0)
            if packed:
                got = got + dot(place[1 + c], flat_rows(ret[t, :, :, ff:ff + half]), 0, 0)
            hid[:, t * ff + c * wide:t * ff + c * wide + wide] = got.astype(BF16)
        span = slice(t * ff, t * ff + ff)
        copies.append(pltpu.make_async_copy(hid.at[:, span], hid_o.at[:, span], sem.at[3 + t]))
        copies[-1].start()
    for copy in copies:
        copy.wait()


def shards(out_grad, routes, pre_act, out_weight, row_factor, col_factor):
    n_dp, n_e = lax.axis_size("dp"), lax.axis_size("expert")
    tok, d = out_grad.shape
    r = pre_act.shape[0]
    ff = out_weight.shape[1]
    slot = r // n_e
    packed = slot > 8
    assert slot <= 12
    kinds = 3 if packed else 1
    assert n_e >= 4 and n_e & (n_e - 1) == 0
    g = n_e // 4
    chunk = next(c for c in (384, 256, 128) if ff % c == 0)
    deep = max(c for c in range(16, 257, 16) if d % c == 0)
    wide_d = up128(d) + d // 2 // 128 * 128 if packed else d
    assert not packed or 2 * d - d // 256 * 256 <= up128(d)
    wide_f = ff + ff // 2 if packed else ff
    vm = pl.BlockSpec(memory_space=pltpu.VMEM)
    hbm = pl.BlockSpec(memory_space=pl.ANY)
    dma = pltpu.SemaphoreType.DMA
    out = pltpu.VMEM
    held = pl.pallas_call(
        functools.partial(kernel, (n_dp, n_e, slot, chunk, deep)),
        out_shape=(out((n_dp, n_e, 8, wide_f), BF16), out((kinds, n_e * 8, tok), BF16),
                   out((1, d, ff), BF16), out((1, ff), F32), out((1, d), F32)),
        in_specs=[hbm] * 6,
        out_specs=(vm,) * 5,
        scratch_shapes=[
            pltpu.VMEM((d, tok), BF16),
            pltpu.VMEM((1, tok), jnp.int32),
            pltpu.VMEM((1, ff), F32),
            pltpu.VMEM((1, d), F32),
            pltpu.VMEM((kinds, g * slot, g * 8), BF16),
            pltpu.VMEM((kinds, g * 8, g * slot), BF16),
            pltpu.VMEM((n_e, 8, wide_d), BF16),
            pltpu.VMEM((n_dp, n_e, 8, wide_d), BF16),
            pltpu.VMEM((n_dp, r, d), BF16),
            pltpu.VMEM((n_dp, r, ff), BF16),
            pltpu.VMEM((d, ff), BF16),
            pltpu.VMEM((d, ff), F32),
            pltpu.VMEM((n_dp, n_e, 8, wide_f), BF16),
            pltpu.VMEM((n_dp, 2, d), F32),
            pltpu.VMEM((2, up128(d), 128), F32),
            pltpu.VMEM((1, up128(d)), F32),
            pltpu.VMEM((up128(d), 128), F32),
            dma((6,)), pltpu.SemaphoreType.REGULAR((n_e.bit_length() - 1,)), dma((1,)), dma((4,)),
            dma((n_dp - 1,)), dma((n_dp - 1, 4)), dma((n_dp - 1,)), dma((n_dp - 1, 4)),
            dma((n_dp,)), dma((n_dp,)), dma((n_dp - 1,)), dma((n_dp - 1,)),
        ],
        compiler_params=pltpu.CompilerParams(
            collective_id=0, has_side_effects=True, vmem_limit_bytes=59 * 1024 * 1024),
    )(out_grad.T, routes.reshape(1, tok), pre_act, jnp.swapaxes(out_weight, 1, 2), row_factor,
      col_factor)
    hid, neww, newrow, newcol = pl.pallas_call(
        functools.partial(finish, packed, ff),
        out_shape=tuple(jax.ShapeDtypeStruct(*x) for x in (
            ((tok, ff * n_dp), BF16), ((1, d, ff), BF16), ((1, ff), F32), ((1, d), F32))),
        in_specs=[vm] * 5,
        out_specs=[hbm] * 4,
        scratch_shapes=[pltpu.VMEM((tok, ff * n_dp), BF16), dma((3 + n_dp,))],
        compiler_params=pltpu.CompilerParams(vmem_limit_bytes=8 * 1024 * 1024),
    )(*held)
    return hid, jnp.swapaxes(neww, 1, 2), newrow, newcol


def solution(mesh):
    placed = (
        P(("dp", "expert"), None),
        P(("dp", "expert"), None),
        P(("dp", "expert"), None),
        P("expert", "dp", None),
        P("expert", "dp"),
        P("expert", None),
    )
    return jax.shard_map(
        shards,
        mesh=mesh,
        in_specs=placed,
        out_specs=(
            P(("dp", "expert"), None),
            P("expert", "dp", None),
            P("expert", "dp"),
            P("expert", None),
        ),
        check_vma=False,
    )
```

```python
import functools
import jax
import jax.numpy as jnp
from jax import lax
from jax.experimental import pallas as pl
from jax.experimental.pallas import tpu as pltpu
from jax.sharding import PartitionSpec as P

MESH = pl.DeviceIdType.MESH
F32, BF16 = jnp.float32, jnp.bfloat16


def up128(n):
    return -(-n // 128) * 128


def dot(a, b, ca=1, cb=0):
    return lax.dot_general(a, b, (((ca,), (cb,)), ((), ())), preferred_element_type=F32)


def onehot(hit):
    return jnp.where(hit, 1.0, 0.0).astype(BF16)


def flat_rows(x):
    return x.astype(F32).reshape(x.shape[0] * 8, x.shape[2]).astype(BF16)


def kernel(cfg, og_h, rrow_h, pre, w, rf_h, cf_h,
           ret, place, neww, newrow, newcol,
           og, rrow, rf, cf, qn, qt,
           dy_out, dy_all, dyn, pre_all, wv, grad, snd, colst, colacc, cspad, cscol,
           loc, flood, dy_s, dy_r, fw_s, fw_r, pre_s, pre_r, rt_s, rt_r, st_s, st_r):
    n_dp, n_e, slot, chunk, deep = cfg
    d, tok = og.shape
    ff = wv.shape[1]
    packed = slot > 8
    half, dp_off, h0 = ff // 2, up128(d), d // 2 // 128 * 128
    rest = d - 2 * h0
    bits = n_e.bit_length() - 1
    g = n_e // 4
    n = g * slot
    i, e = lax.axis_index("dp"), lax.axis_index("expert")
    others = [(o, lax.rem(i + o, n_dp)) for o in range(1, n_dp)]

    def flip(x, b):
        return x + (1 - 2 * lax.rem(lax.div(x, 1 << b), 2)) * (1 << b)

    def loop(count, act):
        def step(k, _):
            act(k)
            return 0
        lax.fori_loop(0, count, step, 0)

    barrier = pltpu.get_barrier_semaphore()
    for _, t in others:
        pl.semaphore_signal(barrier, inc=1, device_id=(t, e), device_id_type=MESH)
    for b in range(bits):
        pl.semaphore_signal(barrier, inc=1, device_id=(i, flip(e, b)), device_id_type=MESH)

    cols = lambda t: pl.ds(pl.multiple_of(t * ff, 128), ff)
    loads = [pltpu.make_async_copy(x, y, loc.at[k]) for k, (x, y) in enumerate((
        (rrow_h, rrow), (og_h, og), (w.at[0], wv), (pre.at[:, cols(i)], pre_all.at[i]), (rf_h, rf),
        (cf_h, cf)))]
    for load in loads:
        load.start()

    def tables(q, rows, cells, axis):
        for k in range(q.shape[0]):
            row = lax.broadcasted_iota(jnp.int32, (rows, cells), axis)
            cell = lax.broadcasted_iota(jnp.int32, (rows, cells), 1 - axis)
            at = cell & 7
            wants = slot * (cell >> 3) + at + (0, 8, 4)[k]
            held = (at < min(slot, 8), at < slot - 8, at >= 4)[k]
            q[k] = onehot((row == wants) & held)

    tables(qn, n, g * 8, 0)
    tables(qt, g * 8, n, 1)

    loads[0].wait()
    named = jnp.broadcast_to(rrow[...].astype(F32), (tok, tok))
    same = named == named.T
    at_row = lax.broadcasted_iota(jnp.int32, (tok, tok), 0)
    at_col = lax.broadcasted_iota(jnp.int32, (tok, tok), 1)
    order = jnp.sum(jnp.where(same & (at_row < at_col), 1.0, 0.0), axis=0, keepdims=True)
    base = rrow[...].astype(F32) * 8.0 + order
    rows = lax.broadcasted_iota(jnp.int32, (n_e * 8, tok), 0).astype(F32)
    place[0] = onehot(rows == jnp.where(order < 8.0, base, -1.0))
    if packed:
        place[1] = onehot(rows == jnp.where(order >= 8.0, base - 8.0, -1.0))
        place[2] = onehot(rows == jnp.where(order >= 8.0, base - 4.0, -1.0))
    loads[1].wait()
    dy_out[:, :, 0:d] = dot(place[0], og[...], 1, 1).reshape(n_e, 8, d).astype(BF16)
    if packed:
        tail = dot(place[1], og[0:h0, :], 1, 1) + dot(place[2], og[h0:2 * h0, :], 1, 1)
        dy_out[:, :, dp_off:dp_off + h0] = tail.reshape(n_e, 8, h0).astype(BF16)
        if rest:
            more = dot(place[1], og[2 * h0:d, :], 1, 1)
            dy_out[:, :, d:d + rest] = more.reshape(n_e, 8, rest).astype(BF16)

    quarter = lax.div(e, g)
    group = {0: quarter, 1: flip(quarter, 0), 2: flip(quarter, 1), 3: flip(flip(quarter, 0), 1)}

    def members(k, act):
        if k:
            loop(g, lambda m: act(group[k] * g + m))
        else:
            loop(g - 1, lambda m: act(quarter * g + lax.rem(e + 1 + m, g)))

    def send_dy(k, t):
        return pltpu.make_async_remote_copy(
            src_ref=dy_out.at[t], dst_ref=dy_all.at[i, e], send_sem=dy_s.at[0],
            recv_sem=dy_r.at[k], device_id=(i, t), device_id_type=MESH)

    def rows_of(k):
        return pl.ds(pl.multiple_of(group[k] * n, 16), n)

    def send_pre(o, t, k):
        return pltpu.make_async_remote_copy(
            src_ref=pre.at[rows_of(k), cols(t)], dst_ref=pre_all.at[i, rows_of(k)],
            send_sem=pre_s.at[o - 1], recv_sem=pre_r.at[n_dp - o - 1, k], device_id=(t, e),
            device_id_type=MESH)

    def send_fw(o, t, k):
        part = pl.ds(group[k] * g, g)
        return pltpu.make_async_remote_copy(
            src_ref=dy_all.at[i, part], dst_ref=dy_all.at[i, part], send_sem=fw_s.at[o - 1],
            recv_sem=fw_r.at[n_dp - o - 1, k], device_id=(t, e), device_id_type=MESH)

    def send_ret(o, t, j):
        return pltpu.make_async_remote_copy(
            src_ref=snd.at[t, j], dst_ref=ret.at[i, e], send_sem=rt_s.at[o],
            recv_sem=rt_r.at[lax.rem(n_dp - o, n_dp)], device_id=(t, j), device_id_type=MESH)

    def send_st(o, t):
        return pltpu.make_async_remote_copy(
            src_ref=colst.at[i], dst_ref=colst.at[i], send_sem=st_s.at[o - 1],
            recv_sem=st_r.at[n_dp - o - 1], device_id=(t, e), device_id_type=MESH)

    def meet(b):
        pl.semaphore_signal(flood.at[b], inc=1, device_id=(i, flip(e, b)), device_id_type=MESH)
        pl.semaphore_wait(flood.at[b], 1)

    with jax.named_scope("bar"):
        pl.semaphore_wait(barrier, bits + n_dp - 1)
    for k in (2, 3, 1, 0):
        for o, t in others:
            send_pre(o, t, k).start()
    across = flip(e, bits - 1)
    send_dy(2, across).start()
    with jax.named_scope("flood"):
        for b in range(bits - 2):
            meet(b)
            first = lax.div(flip(across, b), 1 << b) * (1 << b)
            loop(1 << b, lambda m: send_dy(2, first + m).start())
    with jax.named_scope("flood2"):
        meet(bits - 2)
    for k in (3, 1, 0):
        members(k, lambda t: send_dy(k, t).start())
    own = pltpu.make_async_copy(dy_out.at[e], dy_all.at[i, e], dy_r.at[0])
    own.start()

    colacc[...] = jnp.zeros_like(colacc)

    def back(t, k):
        part = pl.ds(group[k] * g, g)
        where = rows_of(k)
        dy = dot(qn[0], flat_rows(dy_all[t, part, :, 0:d]))
        if packed:
            q_lo, q_hi = qn[1], qn[2]
            tail = flat_rows(dy_all[t, part, :, dp_off:dp_off + h0])
            pieces = [dot(q_lo, tail), dot(q_hi, tail)]
            if rest:
                ends = dot(q_lo, flat_rows(dy_all[t, part, :, 2 * h0:dp_off]))
                pieces.append(ends[:, d - 2 * h0:d - 2 * h0 + rest])
            dy = dy + jnp.concatenate(pieces, axis=1)
        dy = dy.astype(BF16)
        dyn[t, where, :] = dy
        tail = None
        for c in range(2 if packed else 1):
            wide = half if packed else ff
            span = slice(c * wide, c * wide + wide)
            bk = dot(dy, wv[:, span])
            keep = pre_all[t, where, span].astype(F32) > 0.0
            bk = jnp.where(keep, bk, 0.0).astype(BF16)
            snd[t, part, :, span] = dot(qt[0], bk).reshape(g, 8, wide).astype(BF16)
            if packed:
                more = dot(qt[1 + c], bk)
                tail = more if tail is None else tail + more
        if packed:
            snd[t, part, :, ff:ff + half] = tail.reshape(g, 8, half).astype(BF16)

    def arrive(k):
        part = pl.ds(group[k] * g, g)
        with jax.named_scope("recv%d" % k):
            pltpu.make_async_copy(dy_all.at[0, part], dy_all.at[i, part], dy_r.at[k]).wait()

    def forward(k):
        for o, t in others:
            send_fw(o, t, k).start()

    def near(k):
        with jax.named_scope("back%d" % k):
            back(i, k)
        members(k, lambda j: send_ret(0, i, j).start())

    def await_cross(k):
        part = pl.ds(group[k] * g, g)
        for o, t in others:
            with jax.named_scope("waitpre%d" % k):
                pltpu.make_async_copy(
                    pre_all.at[i, rows_of(k)], pre_all.at[t, rows_of(k)], pre_r.at[o - 1, k]).wait()
            with jax.named_scope("waitfw%d" % k):
                pltpu.make_async_copy(dy_all.at[i, part], dy_all.at[t, part], fw_r.at[o - 1, k]).wait()

    def back_cross(k):
        for _, t in others:
            with jax.named_scope("backx%d" % k):
                back(t, k)

    def cross(k):
        await_cross(k)
        back_cross(k)

    def send_cross(k):
        for o, t in others:
            loop(g, lambda m: send_ret(o, t, group[k] * g + m).start())

    arrive(2)
    forward(2)
    loads[2].wait()
    loads[3].wait()
    near(2)
    arrive(3)
    forward(3)
    near(3)
    arrive(1)
    forward(1)
    near(1)
    arrive(0)
    forward(0)
    near(0)
    own_ret = pltpu.make_async_copy(snd.at[i, e], ret.at[i, e], rt_r.at[0])
    own_ret.start()
    cross(2)
    cross(3)
    cross(1)
    send_cross(2)
    send_cross(3)
    await_cross(0)
    send_cross(1)
    back_cross(0)

    loads[4].wait()
    loads[5].wait()

    def gradient(c):
        span = pl.ds(pl.multiple_of(c * chunk, 128), chunk)
        acc = None
        for t in range(n_dp):
            part = dot(dyn[t], jnp.maximum(pre_all[t, :, span], 0), 0, 0)
            acc = part if acc is None else acc + part
        grad[:, span] = acc
        sq = acc * acc
        rn = 0.8 * rf[0:1, span] + 0.2 * (jnp.sum(sq, axis=0, keepdims=True) / d + 1e-30)
        newrow[0:1, span] = rn
        for k, x in enumerate((sq, sq * (1.0 / rn))):
            folded = x[:, 0:128]
            for b in range(1, chunk // 128):
                folded = folded + x[:, b * 128:b * 128 + 128]
            colacc[k, 0:d, :] += folded

    with jax.named_scope("grad"):
        loop(ff // chunk, gradient)
    blocks = [(b, min(b + 128, d)) for b in range(0, d, 128)]
    for k in range(2):
        for lo, hi in blocks:
            sums = jnp.sum(colacc[k, lo:lo + 128, :].T, axis=0, keepdims=True)
            colst[i, k:k + 1, lo:hi] = sums[:, 0:hi - lo]
    for o, t in others:
        send_st(o, t).start()
    send_cross(0)

    with jax.named_scope("waitst"):
        for o, t in others:
            pltpu.make_async_copy(colst.at[i], colst.at[t], st_r.at[o - 1]).wait()
    col, weighted = jnp.zeros((1, d), F32), jnp.zeros((1, d), F32)
    for t in range(n_dp):
        col = col + colst[t, 0:1, :]
        weighted = weighted + colst[t, 1:2, :]
    full = ff * n_dp
    cn = 0.8 * cf[...] + 0.2 * (col / full + 1e-30)
    newcol[...] = cn
    spread = jnp.sqrt(jnp.sum(weighted / cn, axis=1, keepdims=True) / (full * d))
    cspad[...] = jnp.zeros_like(cspad)
    cspad[0:1, 0:d] = lax.rsqrt(cn) / jnp.maximum(1.0, spread / 0.01)
    for lo, hi in blocks:
        cscol[lo:lo + 128, :] = jnp.broadcast_to(cspad[0:1, lo:lo + 128], (128, 128)).T

    def apply(c):
        span = pl.ds(pl.multiple_of(c * deep, 16), deep)
        update = grad[span, :] * lax.rsqrt(newrow[...]) * cscol[span, 0:1]
        neww[0, span, :] = (wv[span, :].astype(F32) - update).astype(BF16)

    with jax.named_scope("apply"):
        loop(d // deep, apply)

    for o, t in [(0, i)] + others:
        with jax.named_scope("waitret%d" % o):
            pltpu.make_async_copy(snd.at[0], ret.at[t], rt_r.at[o]).wait()

    def sent(src, sem):
        pltpu.make_async_copy(src, src, sem).wait()

    with jax.named_scope("sent"):
        sent(dy_out.at[0:n_e - 1], dy_s.at[0])
        sent(snd.at[0, 0:n_e - 1], rt_s.at[0])
        for o, t in others:
            sent(pre_all.at[0], pre_s.at[o - 1])
            sent(dy_all.at[0], fw_s.at[o - 1])
            sent(snd.at[0], rt_s.at[o])
            sent(colst.at[0], st_s.at[o - 1])


def finish(packed, ff, ret, place, neww, newrow, newcol, hid_o, neww_o, newrow_o, newcol_o, hid, sem):
    copies = [pltpu.make_async_copy(x, y, sem.at[k]) for k, (x, y) in enumerate((
        (neww, neww_o), (newrow, newrow_o), (newcol, newcol_o)))]
    for copy in copies:
        copy.start()
    half = ff // 2
    wide = half if packed else ff
    for t in range(ret.shape[0]):
        for c in range(2 if packed else 1):
            got = dot(place[0], flat_rows(ret[t, :, :, c * wide:c * wide + wide]), 0, 0)
            if packed:
                got = got + dot(place[1 + c], flat_rows(ret[t, :, :, ff:ff + half]), 0, 0)
            hid[:, t * ff + c * wide:t * ff + c * wide + wide] = got.astype(BF16)
        span = slice(t * ff, t * ff + ff)
        copies.append(pltpu.make_async_copy(hid.at[:, span], hid_o.at[:, span], sem.at[3 + t]))
        copies[-1].start()
    for copy in copies:
        copy.wait()


def shards(out_grad, routes, pre_act, out_weight, row_factor, col_factor):
    n_dp, n_e = lax.axis_size("dp"), lax.axis_size("expert")
    tok, d = out_grad.shape
    r = pre_act.shape[0]
    ff = out_weight.shape[1]
    slot = r // n_e
    packed = slot > 8
    assert slot <= 12
    kinds = 3 if packed else 1
    assert n_e >= 4 and n_e & (n_e - 1) == 0
    g = n_e // 4
    chunk = next(c for c in (384, 256, 128) if ff % c == 0)
    deep = max(c for c in range(16, 257, 16) if d % c == 0)
    wide_d = up128(d) + d // 2 // 128 * 128 if packed else d
    assert not packed or 2 * d - d // 256 * 256 <= up128(d)
    wide_f = ff + ff // 2 if packed else ff
    vm = pl.BlockSpec(memory_space=pltpu.VMEM)
    hbm = pl.BlockSpec(memory_space=pl.ANY)
    dma = pltpu.SemaphoreType.DMA
    out = pltpu.VMEM
    held = pl.pallas_call(
        functools.partial(kernel, (n_dp, n_e, slot, chunk, deep)),
        out_shape=(out((n_dp, n_e, 8, wide_f), BF16), out((kinds, n_e * 8, tok), BF16),
                   out((1, d, ff), BF16), out((1, ff), F32), out((1, d), F32)),
        in_specs=[hbm] * 6,
        out_specs=(vm,) * 5,
        scratch_shapes=[
            pltpu.VMEM((d, tok), BF16),
            pltpu.VMEM((1, tok), jnp.int32),
            pltpu.VMEM((1, ff), F32),
            pltpu.VMEM((1, d), F32),
            pltpu.VMEM((kinds, g * slot, g * 8), BF16),
            pltpu.VMEM((kinds, g * 8, g * slot), BF16),
            pltpu.VMEM((n_e, 8, wide_d), BF16),
            pltpu.VMEM((n_dp, n_e, 8, wide_d), BF16),
            pltpu.VMEM((n_dp, r, d), BF16),
            pltpu.VMEM((n_dp, r, ff), BF16),
            pltpu.VMEM((d, ff), BF16),
            pltpu.VMEM((d, ff), F32),
            pltpu.VMEM((n_dp, n_e, 8, wide_f), BF16),
            pltpu.VMEM((n_dp, 2, d), F32),
            pltpu.VMEM((2, up128(d), 128), F32),
            pltpu.VMEM((1, up128(d)), F32),
            pltpu.VMEM((up128(d), 128), F32),
            dma((6,)), pltpu.SemaphoreType.REGULAR((n_e.bit_length() - 1,)), dma((1,)), dma((4,)),
            dma((n_dp - 1,)), dma((n_dp - 1, 4)), dma((n_dp - 1,)), dma((n_dp - 1, 4)),
            dma((n_dp,)), dma((n_dp,)), dma((n_dp - 1,)), dma((n_dp - 1,)),
        ],
        compiler_params=pltpu.CompilerParams(
            collective_id=0, has_side_effects=True, vmem_limit_bytes=59 * 1024 * 1024),
    )(out_grad.T, routes.reshape(1, tok), pre_act, jnp.swapaxes(out_weight, 1, 2), row_factor,
      col_factor)
    hid, neww, newrow, newcol = pl.pallas_call(
        functools.partial(finish, packed, ff),
        out_shape=tuple(jax.ShapeDtypeStruct(*x) for x in (
            ((tok, ff * n_dp), BF16), ((1, d, ff), BF16), ((1, ff), F32), ((1, d), F32))),
        in_specs=[vm] * 5,
        out_specs=[hbm] * 4,
        scratch_shapes=[pltpu.VMEM((tok, ff * n_dp), BF16), dma((3 + n_dp,))],
        compiler_params=pltpu.CompilerParams(vmem_limit_bytes=8 * 1024 * 1024),
    )(*held)
    return hid, jnp.swapaxes(neww, 1, 2), newrow, newcol


def solution(mesh):
    placed = (
        P(("dp", "expert"), None),
        P(("dp", "expert"), None),
        P(("dp", "expert"), None),
        P("expert", "dp", None),
        P("expert", "dp"),
        P("expert", None),
    )
    return jax.shard_map(
        shards,
        mesh=mesh,
        in_specs=placed,
        out_specs=(
            P(("dp", "expert"), None),
            P("expert", "dp", None),
            P("expert", "dp"),
            P("expert", None),
        ),
        check_vma=False,
    )
```

```python
import functools
import jax
import jax.numpy as jnp
from jax import lax
from jax.experimental import pallas as pl
from jax.experimental.pallas import tpu as pltpu
from jax.sharding import PartitionSpec as P

MESH = pl.DeviceIdType.MESH
F32, BF16 = jnp.float32, jnp.bfloat16


def up128(n):
    return -(-n // 128) * 128


def dot(a, b, ca=1, cb=0):
    return lax.dot_general(a, b, (((ca,), (cb,)), ((), ())), preferred_element_type=F32)


def onehot(hit):
    return jnp.where(hit, 1.0, 0.0).astype(BF16)


def flat_rows(x):
    return x.astype(F32).reshape(x.shape[0] * 8, x.shape[2]).astype(BF16)


def kernel(cfg, og_h, rrow_h, pre, w, rf_h, cf_h,
           ret, place, neww, newrow, newcol,
           og, rrow, rf, cf, qn, qt, eye, ends,
           dy_out, dy_all, dyn, pre_all, wv, grad, snd, colst, colacc, cspad, cscol,
           loc, flood, dy_s, dy_r, fw_s, fw_r, pre_s, pre_r, rt_s, rt_r, st_s, st_r):
    n_dp, n_e, slot, chunk, deep = cfg
    d, tok = og.shape
    ff = wv.shape[1]
    packed = slot > 8
    half, dp_off, h0 = ff // 2, up128(d), d // 2 // 128 * 128
    rest = d - 2 * h0
    main, last = d // 128 * 128, d % 128
    bits = n_e.bit_length() - 1
    g = n_e // 4
    n = g * slot
    i, e = lax.axis_index("dp"), lax.axis_index("expert")
    others = [(o, lax.rem(i + o, n_dp)) for o in range(1, n_dp)]

    def flip(x, b):
        return x + (1 - 2 * lax.rem(lax.div(x, 1 << b), 2)) * (1 << b)

    def loop(count, act):
        def step(k, _):
            act(k)
            return 0
        lax.fori_loop(0, count, step, 0)

    barrier = pltpu.get_barrier_semaphore()
    for _, t in others:
        pl.semaphore_signal(barrier, inc=1, device_id=(t, e), device_id_type=MESH)
    for b in range(bits):
        pl.semaphore_signal(barrier, inc=1, device_id=(i, flip(e, b)), device_id_type=MESH)

    cols = lambda t: pl.ds(pl.multiple_of(t * ff, 128), ff)
    loads = [pltpu.make_async_copy(x, y, loc.at[k]) for k, (x, y) in enumerate((
        (rrow_h, rrow), (og_h, og), (w.at[0], wv), (pre.at[:, cols(i)], pre_all.at[i]), (rf_h, rf),
        (cf_h, cf)))]
    for load in loads:
        load.start()

    def tables(q, rows, cells, axis):
        for k in range(q.shape[0]):
            row = lax.broadcasted_iota(jnp.int32, (rows, cells), axis)
            cell = lax.broadcasted_iota(jnp.int32, (rows, cells), 1 - axis)
            at = cell & 7
            wants = slot * (cell >> 3) + at + (0, 8, 4)[k]
            held = (at < min(slot, 8), at < slot - 8, at >= 4)[k]
            q[k] = onehot((row == wants) & held)

    tables(qn, n, g * 8, 0)
    tables(qt, g * 8, n, 1)
    if last:
        eye[...] = onehot(lax.broadcasted_iota(jnp.int32, (n, 128), 0)
                          == lax.broadcasted_iota(jnp.int32, (n, 128), 1))

    loads[0].wait()
    named = jnp.broadcast_to(rrow[...].astype(F32), (tok, tok))
    same = named == named.T
    at_row = lax.broadcasted_iota(jnp.int32, (tok, tok), 0)
    at_col = lax.broadcasted_iota(jnp.int32, (tok, tok), 1)
    order = jnp.sum(jnp.where(same & (at_row < at_col), 1.0, 0.0), axis=0, keepdims=True)
    base = rrow[...].astype(F32) * 8.0 + order
    rows = lax.broadcasted_iota(jnp.int32, (n_e * 8, tok), 0).astype(F32)
    place[0] = onehot(rows == jnp.where(order < 8.0, base, -1.0))
    if packed:
        place[1] = onehot(rows == jnp.where(order >= 8.0, base - 8.0, -1.0))
        place[2] = onehot(rows == jnp.where(order >= 8.0, base - 4.0, -1.0))
    loads[1].wait()
    dy_out[:, :, 0:d] = dot(place[0], og[...], 1, 1).reshape(n_e, 8, d).astype(BF16)
    if packed:
        tail = dot(place[1], og[0:h0, :], 1, 1) + dot(place[2], og[h0:2 * h0, :], 1, 1)
        dy_out[:, :, dp_off:dp_off + h0] = tail.reshape(n_e, 8, h0).astype(BF16)
        if rest:
            more = dot(place[1], og[2 * h0:d, :], 1, 1)
            dy_out[:, :, d:d + rest] = more.reshape(n_e, 8, rest).astype(BF16)

    quarter = lax.div(e, g)
    inner = lax.rem(quarter + 1, 4) >= 2
    outer = lax.rem(quarter + 1, 4) < 2
    group = {0: quarter, 1: flip(quarter, 0), 2: flip(quarter, 1), 3: flip(flip(quarter, 0), 1)}

    def members(k, act):
        if k:
            loop(g, lambda m: act(group[k] * g + m))
        else:
            loop(g - 1, lambda m: act(quarter * g + lax.rem(e + 1 + m, g)))

    def send_dy(k, t):
        return pltpu.make_async_remote_copy(
            src_ref=dy_out.at[t], dst_ref=dy_all.at[e], send_sem=dy_s.at[0],
            recv_sem=dy_r.at[k], device_id=(i, t), device_id_type=MESH)

    def rows_of(k):
        return pl.ds(pl.multiple_of(group[k] * n, 16), n)

    def send_pre(o, t, k):
        return pltpu.make_async_remote_copy(
            src_ref=pre.at[rows_of(k), cols(t)], dst_ref=pre_all.at[i, rows_of(k)],
            send_sem=pre_s.at[o - 1], recv_sem=pre_r.at[n_dp - o - 1, k], device_id=(t, e),
            device_id_type=MESH)

    def send_fw(o, t, k):
        refs = [dyn.at[i, rows_of(k), 0:main]] + ([ends.at[i, group[k]]] if last else [])
        return [pltpu.make_async_remote_copy(
            src_ref=x, dst_ref=x, send_sem=fw_s.at[o - 1, m], recv_sem=fw_r.at[n_dp - o - 1, k, m],
            device_id=(t, e), device_id_type=MESH) for m, x in enumerate(refs)]

    def send_ret(o, t, j):
        return pltpu.make_async_remote_copy(
            src_ref=snd.at[t, j], dst_ref=ret.at[i, e], send_sem=rt_s.at[o],
            recv_sem=rt_r.at[lax.rem(n_dp - o, n_dp)], device_id=(t, j), device_id_type=MESH)

    def send_st(o, t):
        return pltpu.make_async_remote_copy(
            src_ref=colst.at[i], dst_ref=colst.at[i], send_sem=st_s.at[o - 1],
            recv_sem=st_r.at[n_dp - o - 1], device_id=(t, e), device_id_type=MESH)

    def meet(b):
        pl.semaphore_signal(flood.at[b], inc=1, device_id=(i, flip(e, b)), device_id_type=MESH)
        pl.semaphore_wait(flood.at[b], 1)

    with jax.named_scope("bar"):
        pl.semaphore_wait(barrier, bits + n_dp - 1)
    for k in (2, 3, 1, 0):
        for o, t in others:
            send_pre(o, t, k).start()
    across = flip(e, bits - 1)
    send_dy(2, across).start()
    with jax.named_scope("flood"):
        for b in range(bits - 2):
            meet(b)
            first = lax.div(flip(across, b), 1 << b) * (1 << b)
            loop(1 << b, lambda m: send_dy(2, first + m).start())
    with jax.named_scope("flood2"):
        meet(bits - 2)
    for k in (3, 1, 0):
        members(k, lambda t: send_dy(k, t).start())
    own = pltpu.make_async_copy(dy_out.at[e], dy_all.at[e], dy_r.at[0])
    own.start()

    colacc[...] = jnp.zeros_like(colacc)

    def unpack(k):
        part = pl.ds(group[k] * g, g)
        dy = dot(qn[0], flat_rows(dy_all[part, :, 0:d]))
        if packed:
            q_lo, q_hi = qn[1], qn[2]
            tail = flat_rows(dy_all[part, :, dp_off:dp_off + h0])
            pieces = [dot(q_lo, tail), dot(q_hi, tail)]
            if rest:
                more = dot(q_lo, flat_rows(dy_all[part, :, 2 * h0:dp_off]))
                pieces.append(more[:, d - 2 * h0:d - 2 * h0 + rest])
            dy = dy + jnp.concatenate(pieces, axis=1)
        dy = dy.astype(BF16)
        dyn[i, rows_of(k), :] = dy
        if last:
            ends[i, group[k]] = dot(dy[:, main:d], eye[...], 0, 0).astype(BF16)
        return dy

    def back(t, k, dy):
        part = pl.ds(group[k] * g, g)
        where = rows_of(k)
        tail = None
        for c in range(2 if packed else 1):
            wide = half if packed else ff
            span = slice(c * wide, c * wide + wide)
            bk = dot(dy, wv[:, span])
            keep = pre_all[t, where, span].astype(F32) > 0.0
            bk = jnp.where(keep, bk, 0.0).astype(BF16)
            snd[t, part, :, span] = dot(qt[0], bk).reshape(g, 8, wide).astype(BF16)
            if packed:
                more = dot(qt[1 + c], bk)
                tail = more if tail is None else tail + more
        if packed:
            snd[t, part, :, ff:ff + half] = tail.reshape(g, 8, half).astype(BF16)

    def arrive(k):
        part = pl.ds(group[k] * g, g)
        with jax.named_scope("recv%d" % k):
            pltpu.make_async_copy(dy_out.at[part], dy_all.at[part], dy_r.at[k]).wait()

    def forward(k):
        for o, t in others:
            for copy in send_fw(o, t, k):
                copy.start()

    def near(k):
        with jax.named_scope("back%d" % k):
            back(i, k, unpack(k))
        members(k, lambda j: send_ret(0, i, j).start())

    def await_cross(k):
        for o, t in others:
            with jax.named_scope("waitpre%d" % k):
                pltpu.make_async_copy(
                    pre_all.at[i, rows_of(k)], pre_all.at[t, rows_of(k)], pre_r.at[o - 1, k]).wait()
            with jax.named_scope("waitfw%d" % k):
                rows = dyn.at[t, rows_of(k), 0:main]
                pltpu.make_async_copy(rows, rows, fw_r.at[o - 1, k, 0]).wait()
                if last:
                    tile = ends.at[t, group[k]]
                    pltpu.make_async_copy(tile, tile, fw_r.at[o - 1, k, 1]).wait()
                    dyn[t, rows_of(k), main:d] = dot(eye[...], ends[t, group[k]], 1, 1).astype(BF16)

    def back_cross(k):
        for _, t in others:
            with jax.named_scope("backx%d" % k):
                back(t, k, dyn[t, rows_of(k), :])

    def cross(k):
        await_cross(k)
        back_cross(k)

    def send_cross(k, first=0, count=g):
        for o, t in others:
            loop(count, lambda m: send_ret(o, t, group[k] * g + first + m).start())

    arrive(2)
    loads[2].wait()
    loads[3].wait()
    near(2)
    forward(2)
    arrive(3)
    near(3)
    forward(3)
    arrive(1)
    near(1)
    forward(1)
    arrive(0)
    near(0)
    forward(0)
    own_ret = pltpu.make_async_copy(snd.at[i, e], ret.at[i, e], rt_r.at[0])
    own_ret.start()
    def gradient_own(c):
        span = pl.ds(pl.multiple_of(c * chunk, 128), chunk)
        grad[:, span] = dot(dyn[i], jnp.maximum(pre_all[i, :, span], 0), 0, 0)

    with jax.named_scope("gradown"):
        loop(ff // chunk, gradient_own)
    cross(2)
    cross(3)
    cross(1)
    send_cross(2)
    send_cross(3)
    await_cross(0)
    @pl.when(inner)
    def _():
        send_cross(1)

    back_cross(0)
    @pl.when(inner)
    def _():
        send_cross(0, 0, g // 2)


    loads[4].wait()
    loads[5].wait()

    def gradient(c):
        span = pl.ds(pl.multiple_of(c * chunk, 128), chunk)
        acc = grad[:, span]
        for _, t in others:
            acc = acc + dot(dyn[t], jnp.maximum(pre_all[t, :, span], 0), 0, 0)
        grad[:, span] = acc
        sq = acc * acc
        rn = 0.8 * rf[0:1, span] + 0.2 * (jnp.sum(sq, axis=0, keepdims=True) / d + 1e-30)
        newrow[0:1, span] = rn
        for k, x in enumerate((sq, sq * (1.0 / rn))):
            folded = x[:, 0:128]
            for b in range(1, chunk // 128):
                folded = folded + x[:, b * 128:b * 128 + 128]
            colacc[k, 0:d, :] += folded

    with jax.named_scope("grad"):
        loop(ff // chunk, gradient)
    blocks = [(b, min(b + 128, d)) for b in range(0, d, 128)]
    for k in range(2):
        for lo, hi in blocks:
            sums = jnp.sum(colacc[k, lo:lo + 128, :].T, axis=0, keepdims=True)
            colst[i, k:k + 1, lo:hi] = sums[:, 0:hi - lo]
    for o, t in others:
        send_st(o, t).start()
    @pl.when(outer)
    def _():
        send_cross(1)

    @pl.when(inner)
    def _():
        send_cross(0, g // 2, g // 2)

    @pl.when(jnp.logical_not(inner))
    def _():
        send_cross(0)


    with jax.named_scope("waitst"):
        for o, t in others:
            pltpu.make_async_copy(colst.at[i], colst.at[t], st_r.at[o - 1]).wait()
    col, weighted = jnp.zeros((1, d), F32), jnp.zeros((1, d), F32)
    for t in range(n_dp):
        col = col + colst[t, 0:1, :]
        weighted = weighted + colst[t, 1:2, :]
    full = ff * n_dp
    cn = 0.8 * cf[...] + 0.2 * (col / full + 1e-30)
    newcol[...] = cn
    spread = jnp.sqrt(jnp.sum(weighted / cn, axis=1, keepdims=True) / (full * d))
    cspad[...] = jnp.zeros_like(cspad)
    cspad[0:1, 0:d] = lax.rsqrt(cn) / jnp.maximum(1.0, spread / 0.01)
    for lo, hi in blocks:
        cscol[lo:lo + 128, :] = jnp.broadcast_to(cspad[0:1, lo:lo + 128], (128, 128)).T

    def apply(c):
        span = pl.ds(pl.multiple_of(c * deep, 16), deep)
        update = grad[span, :] * lax.rsqrt(newrow[...]) * cscol[span, 0:1]
        neww[0, span, :] = (wv[span, :].astype(F32) - update).astype(BF16)

    with jax.named_scope("apply"):
        loop(d // deep, apply)

    for o, t in [(0, i)] + others:
        with jax.named_scope("waitret%d" % o):
            pltpu.make_async_copy(snd.at[0], ret.at[t], rt_r.at[o]).wait()

    def sent(src, sem):
        pltpu.make_async_copy(src, src, sem).wait()

    with jax.named_scope("sent"):
        sent(dy_out.at[0:n_e - 1], dy_s.at[0])
        sent(snd.at[0, 0:n_e - 1], rt_s.at[0])
        for o, t in others:
            sent(pre_all.at[0], pre_s.at[o - 1])
            sent(dyn.at[0, :, 0:main], fw_s.at[o - 1, 0])
            if last:
                sent(ends.at[0], fw_s.at[o - 1, 1])
            sent(snd.at[0], rt_s.at[o])
            sent(colst.at[0], st_s.at[o - 1])


def finish(packed, ff, ret, place, neww, newrow, newcol, hid_o, neww_o, newrow_o, newcol_o, hid, sem):
    copies = [pltpu.make_async_copy(x, y, sem.at[k]) for k, (x, y) in enumerate((
        (neww, neww_o), (newrow, newrow_o), (newcol, newcol_o)))]
    for copy in copies:
        copy.start()
    half = ff // 2
    wide = half if packed else ff
    for t in range(ret.shape[0]):
        for c in range(2 if packed else 1):
            got = dot(place[0], flat_rows(ret[t, :, :, c * wide:c * wide + wide]), 0, 0)
            if packed:
                got = got + dot(place[1 + c], flat_rows(ret[t, :, :, ff:ff + half]), 0, 0)
            hid[:, t * ff + c * wide:t * ff + c * wide + wide] = got.astype(BF16)
        span = slice(t * ff, t * ff + ff)
        copies.append(pltpu.make_async_copy(hid.at[:, span], hid_o.at[:, span], sem.at[3 + t]))
        copies[-1].start()
    for copy in copies:
        copy.wait()


def shards(out_grad, routes, pre_act, out_weight, row_factor, col_factor):
    n_dp, n_e = lax.axis_size("dp"), lax.axis_size("expert")
    tok, d = out_grad.shape
    r = pre_act.shape[0]
    ff = out_weight.shape[1]
    slot = r // n_e
    packed = slot > 8
    assert slot <= 12
    kinds = 3 if packed else 1
    assert n_e >= 4 and n_e & (n_e - 1) == 0
    g = n_e // 4
    assert g * slot <= 128
    chunk = next(c for c in (384, 256, 128) if ff % c == 0)
    deep = max(c for c in range(16, 257, 16) if d % c == 0)
    wide_d = up128(d) + d // 2 // 128 * 128 if packed else d
    assert not packed or 2 * d - d // 256 * 256 <= up128(d)
    wide_f = ff + ff // 2 if packed else ff
    vm = pl.BlockSpec(memory_space=pltpu.VMEM)
    hbm = pl.BlockSpec(memory_space=pl.ANY)
    dma = pltpu.SemaphoreType.DMA
    out = pltpu.VMEM
    held = pl.pallas_call(
        functools.partial(kernel, (n_dp, n_e, slot, chunk, deep)),
        out_shape=(out((n_dp, n_e, 8, wide_f), BF16), out((kinds, n_e * 8, tok), BF16),
                   out((1, d, ff), BF16), out((1, ff), F32), out((1, d), F32)),
        in_specs=[hbm] * 6,
        out_specs=(vm,) * 5,
        scratch_shapes=[
            pltpu.VMEM((d, tok), BF16),
            pltpu.VMEM((1, tok), jnp.int32),
            pltpu.VMEM((1, ff), F32),
            pltpu.VMEM((1, d), F32),
            pltpu.VMEM((kinds, g * slot, g * 8), BF16),
            pltpu.VMEM((kinds, g * 8, g * slot), BF16),
            pltpu.VMEM((g * slot, 128), BF16),
            pltpu.VMEM((n_dp, 4, max(d % 128, 1), 128), BF16),
            pltpu.VMEM((n_e, 8, wide_d), BF16),
            pltpu.VMEM((n_e, 8, wide_d), BF16),
            pltpu.VMEM((n_dp, r, d), BF16),
            pltpu.VMEM((n_dp, r, ff), BF16),
            pltpu.VMEM((d, ff), BF16),
            pltpu.VMEM((d, ff), F32),
            pltpu.VMEM((n_dp, n_e, 8, wide_f), BF16),
            pltpu.VMEM((n_dp, 2, d), F32),
            pltpu.VMEM((2, up128(d), 128), F32),
            pltpu.VMEM((1, up128(d)), F32),
            pltpu.VMEM((up128(d), 128), F32),
            dma((6,)), pltpu.SemaphoreType.REGULAR((n_e.bit_length() - 1,)), dma((1,)), dma((4,)),
            dma((n_dp - 1, 2)), dma((n_dp - 1, 4, 2)), dma((n_dp - 1,)), dma((n_dp - 1, 4)),
            dma((n_dp,)), dma((n_dp,)), dma((n_dp - 1,)), dma((n_dp - 1,)),
        ],
        compiler_params=pltpu.CompilerParams(
            collective_id=0, has_side_effects=True, vmem_limit_bytes=59 * 1024 * 1024),
    )(out_grad.T, routes.reshape(1, tok), pre_act, jnp.swapaxes(out_weight, 1, 2), row_factor,
      col_factor)
    hid, neww, newrow, newcol = pl.pallas_call(
        functools.partial(finish, packed, ff),
        out_shape=tuple(jax.ShapeDtypeStruct(*x) for x in (
            ((tok, ff * n_dp), BF16), ((1, d, ff), BF16), ((1, ff), F32), ((1, d), F32))),
        in_specs=[vm] * 5,
        out_specs=[hbm] * 4,
        scratch_shapes=[pltpu.VMEM((tok, ff * n_dp), BF16), dma((3 + n_dp,))],
        compiler_params=pltpu.CompilerParams(vmem_limit_bytes=8 * 1024 * 1024),
    )(*held)
    return hid, jnp.swapaxes(neww, 1, 2), newrow, newcol


def solution(mesh):
    placed = (
        P(("dp", "expert"), None),
        P(("dp", "expert"), None),
        P(("dp", "expert"), None),
        P("expert", "dp", None),
        P("expert", "dp"),
        P("expert", None),
    )
    return jax.shard_map(
        shards,
        mesh=mesh,
        in_specs=placed,
        out_specs=(
            P(("dp", "expert"), None),
            P("expert", "dp", None),
            P("expert", "dp"),
            P("expert", None),
        ),
        check_vma=False,
    )
```

```python
import functools
import jax
import jax.numpy as jnp
from jax import lax
from jax.experimental import pallas as pl
from jax.experimental.pallas import tpu as pltpu
from jax.sharding import PartitionSpec as P

MESH = pl.DeviceIdType.MESH
F32, BF16 = jnp.float32, jnp.bfloat16


def up128(n):
    return -(-n // 128) * 128


def dot(a, b, ca=1, cb=0):
    return lax.dot_general(a, b, (((ca,), (cb,)), ((), ())), preferred_element_type=F32)


def onehot(hit):
    return jnp.where(hit, 1.0, 0.0).astype(BF16)


def flat_rows(x):
    return x.astype(F32).reshape(x.shape[0] * 8, x.shape[2]).astype(BF16)


def kernel(cfg, og_h, rrow_h, pre, w, rf_h, cf_h,
           ret, place, neww, newrow, newcol,
           og, rrow, rf, cf, qn, qt, eye, ends,
           dy_out, dy_all, dyn, pre_all, wv, grad, snd, colst, colacc, cspad, cscol,
           loc, flood, dy_s, dy_r, fw_s, fw_r, pre_s, pre_r, rt_s, rt_r, st_s, st_r):
    n_dp, n_e, slot, chunk, deep = cfg
    d, tok = og.shape
    ff = wv.shape[1]
    packed = slot > 8
    half, dp_off, h0 = ff // 2, up128(d), d // 2 // 128 * 128
    rest = d - 2 * h0
    main, last = d // 128 * 128, d % 128
    bits = n_e.bit_length() - 1
    g = n_e // 4
    n = g * slot
    i, e = lax.axis_index("dp"), lax.axis_index("expert")
    others = [(o, lax.rem(i + o, n_dp)) for o in range(1, n_dp)]

    def flip(x, b):
        return x + (1 - 2 * lax.rem(lax.div(x, 1 << b), 2)) * (1 << b)

    def loop(count, act):
        def step(k, _):
            act(k)
            return 0
        lax.fori_loop(0, count, step, 0)

    barrier = pltpu.get_barrier_semaphore()
    for _, t in others:
        pl.semaphore_signal(barrier, inc=1, device_id=(t, e), device_id_type=MESH)
    for b in range(bits):
        pl.semaphore_signal(barrier, inc=1, device_id=(i, flip(e, b)), device_id_type=MESH)

    cols = lambda t: pl.ds(pl.multiple_of(t * ff, 128), ff)
    loads = [pltpu.make_async_copy(x, y, loc.at[k]) for k, (x, y) in enumerate((
        (rrow_h, rrow), (og_h, og), (w.at[0], wv), (pre.at[:, cols(i)], pre_all.at[i]), (rf_h, rf),
        (cf_h, cf)))]
    for load in loads:
        load.start()

    def tables(q, rows, cells, axis):
        for k in range(q.shape[0]):
            row = lax.broadcasted_iota(jnp.int32, (rows, cells), axis)
            cell = lax.broadcasted_iota(jnp.int32, (rows, cells), 1 - axis)
            at = cell & 7
            wants = slot * (cell >> 3) + at + (0, 8, 4)[k]
            held = (at < min(slot, 8), at < slot - 8, at >= 4)[k]
            q[k] = onehot((row == wants) & held)

    tables(qn, n, g * 8, 0)
    tables(qt, g * 8, n, 1)
    if last:
        eye[...] = onehot(lax.broadcasted_iota(jnp.int32, (n, 128), 0)
                          == lax.broadcasted_iota(jnp.int32, (n, 128), 1))

    loads[0].wait()
    named = jnp.broadcast_to(rrow[...].astype(F32), (tok, tok))
    same = named == named.T
    at_row = lax.broadcasted_iota(jnp.int32, (tok, tok), 0)
    at_col = lax.broadcasted_iota(jnp.int32, (tok, tok), 1)
    order = jnp.sum(jnp.where(same & (at_row < at_col), 1.0, 0.0), axis=0, keepdims=True)
    base = rrow[...].astype(F32) * 8.0 + order
    rows = lax.broadcasted_iota(jnp.int32, (n_e * 8, tok), 0).astype(F32)
    place[0] = onehot(rows == jnp.where(order < 8.0, base, -1.0))
    if packed:
        place[1] = onehot(rows == jnp.where(order >= 8.0, base - 8.0, -1.0))
        place[2] = onehot(rows == jnp.where(order >= 8.0, base - 4.0, -1.0))
    loads[1].wait()
    dy_out[:, :, 0:d] = dot(place[0], og[...], 1, 1).reshape(n_e, 8, d).astype(BF16)
    if packed:
        tail = dot(place[1], og[0:h0, :], 1, 1) + dot(place[2], og[h0:2 * h0, :], 1, 1)
        dy_out[:, :, dp_off:dp_off + h0] = tail.reshape(n_e, 8, h0).astype(BF16)
        if rest:
            more = dot(place[1], og[2 * h0:d, :], 1, 1)
            dy_out[:, :, d:d + rest] = more.reshape(n_e, 8, rest).astype(BF16)

    quarter = lax.div(e, g)
    inner = lax.rem(quarter + 1, 4) >= 2
    outer = lax.rem(quarter + 1, 4) < 2
    group = {0: quarter, 1: flip(quarter, 0), 2: flip(quarter, 1), 3: flip(flip(quarter, 0), 1)}

    def members(k, act):
        if k:
            loop(g, lambda m: act(group[k] * g + m))
        else:
            loop(g - 1, lambda m: act(quarter * g + lax.rem(e + 1 + m, g)))

    def send_dy(k, t):
        return pltpu.make_async_remote_copy(
            src_ref=dy_out.at[t], dst_ref=dy_all.at[e], send_sem=dy_s.at[0],
            recv_sem=dy_r.at[k], device_id=(i, t), device_id_type=MESH)

    def rows_of(k):
        return pl.ds(pl.multiple_of(group[k] * n, 16), n)

    def send_pre(o, t):
        return pltpu.make_async_remote_copy(
            src_ref=pre.at[:, cols(t)], dst_ref=pre_all.at[i],
            send_sem=pre_s.at[o - 1], recv_sem=pre_r.at[n_dp - o - 1], device_id=(t, e),
            device_id_type=MESH)

    def send_fw(o, t, k):
        refs = [dyn.at[i, rows_of(k), 0:main]] + ([ends.at[i, group[k]]] if last else [])
        return [pltpu.make_async_remote_copy(
            src_ref=x, dst_ref=x, send_sem=fw_s.at[o - 1, m], recv_sem=fw_r.at[n_dp - o - 1, k, m],
            device_id=(t, e), device_id_type=MESH) for m, x in enumerate(refs)]

    def send_ret(o, t, j):
        return pltpu.make_async_remote_copy(
            src_ref=snd.at[t, j], dst_ref=ret.at[i, e], send_sem=rt_s.at[o],
            recv_sem=rt_r.at[lax.rem(n_dp - o, n_dp)], device_id=(t, j), device_id_type=MESH)

    def send_st(o, t):
        return pltpu.make_async_remote_copy(
            src_ref=colst.at[i], dst_ref=colst.at[i], send_sem=st_s.at[o - 1],
            recv_sem=st_r.at[n_dp - o - 1], device_id=(t, e), device_id_type=MESH)

    def meet(b):
        pl.semaphore_signal(flood.at[b], inc=1, device_id=(i, flip(e, b)), device_id_type=MESH)
        pl.semaphore_wait(flood.at[b], 1)

    with jax.named_scope("bar"):
        pl.semaphore_wait(barrier, bits + n_dp - 1)
    for o, t in others:
        send_pre(o, t).start()
    across = flip(e, bits - 1)
    send_dy(2, across).start()
    with jax.named_scope("flood"):
        for b in range(bits - 2):
            meet(b)
            first = lax.div(flip(across, b), 1 << b) * (1 << b)
            loop(1 << b, lambda m: send_dy(2, first + m).start())
    with jax.named_scope("flood2"):
        meet(bits - 2)
    for k in (3, 1, 0):
        members(k, lambda t: send_dy(k, t).start())
    own = pltpu.make_async_copy(dy_out.at[e], dy_all.at[e], dy_r.at[0])
    own.start()

    colacc[...] = jnp.zeros_like(colacc)

    def unpack(k):
        part = pl.ds(group[k] * g, g)
        dy = dot(qn[0], flat_rows(dy_all[part, :, 0:d]))
        if packed:
            q_lo, q_hi = qn[1], qn[2]
            tail = flat_rows(dy_all[part, :, dp_off:dp_off + h0])
            pieces = [dot(q_lo, tail), dot(q_hi, tail)]
            if rest:
                more = dot(q_lo, flat_rows(dy_all[part, :, 2 * h0:dp_off]))
                pieces.append(more[:, d - 2 * h0:d - 2 * h0 + rest])
            dy = dy + jnp.concatenate(pieces, axis=1)
        dy = dy.astype(BF16)
        dyn[i, rows_of(k), :] = dy
        if last:
            ends[i, group[k]] = dot(dy[:, main:d], eye[...], 0, 0).astype(BF16)
        return dy

    def back(t, k, dy):
        part = pl.ds(group[k] * g, g)
        where = rows_of(k)
        tail = None
        for c in range(2 if packed else 1):
            wide = half if packed else ff
            span = slice(c * wide, c * wide + wide)
            bk = dot(dy, wv[:, span])
            keep = pre_all[t, where, span].astype(F32) > 0.0
            bk = jnp.where(keep, bk, 0.0).astype(BF16)
            snd[t, part, :, span] = dot(qt[0], bk).reshape(g, 8, wide).astype(BF16)
            if packed:
                more = dot(qt[1 + c], bk)
                tail = more if tail is None else tail + more
        if packed:
            snd[t, part, :, ff:ff + half] = tail.reshape(g, 8, half).astype(BF16)

    def arrive(k):
        part = pl.ds(group[k] * g, g)
        with jax.named_scope("recv%d" % k):
            pltpu.make_async_copy(dy_out.at[part], dy_all.at[part], dy_r.at[k]).wait()

    def forward(k):
        for o, t in others:
            for copy in send_fw(o, t, k):
                copy.start()

    def near(k):
        with jax.named_scope("back%d" % k):
            back(i, k, unpack(k))
        members(k, lambda j: send_ret(0, i, j).start())

    def await_cross(k):
        for o, t in others:
            with jax.named_scope("waitfw%d" % k):
                rows = dyn.at[t, rows_of(k), 0:main]
                pltpu.make_async_copy(rows, rows, fw_r.at[o - 1, k, 0]).wait()
                if last:
                    tile = ends.at[t, group[k]]
                    pltpu.make_async_copy(tile, tile, fw_r.at[o - 1, k, 1]).wait()
                    dyn[t, rows_of(k), main:d] = dot(eye[...], ends[t, group[k]], 1, 1).astype(BF16)

    def back_cross(k):
        for _, t in others:
            with jax.named_scope("backx%d" % k):
                back(t, k, dyn[t, rows_of(k), :])

    def cross(k):
        await_cross(k)
        back_cross(k)

    def send_cross(k, first=0, count=g):
        for o, t in others:
            loop(count, lambda m: send_ret(o, t, group[k] * g + first + m).start())

    arrive(2)
    loads[2].wait()
    loads[3].wait()
    near(2)
    forward(2)
    arrive(3)
    near(3)
    forward(3)
    arrive(1)
    near(1)
    forward(1)
    arrive(0)
    near(0)
    forward(0)
    own_ret = pltpu.make_async_copy(snd.at[i, e], ret.at[i, e], rt_r.at[0])
    own_ret.start()
    def gradient_own(c):
        span = pl.ds(pl.multiple_of(c * chunk, 128), chunk)
        grad[:, span] = dot(dyn[i], jnp.maximum(pre_all[i, :, span], 0), 0, 0)

    with jax.named_scope("gradown"):
        loop(ff // chunk, gradient_own)
    for o, t in others:
        pltpu.make_async_copy(pre_all.at[i], pre_all.at[t], pre_r.at[o - 1]).wait()
    cross(2)
    cross(3)
    cross(1)
    send_cross(2)
    send_cross(3)
    await_cross(0)
    @pl.when(inner)
    def _():
        send_cross(1)

    back_cross(0)
    @pl.when(inner)
    def _():
        send_cross(0, 0, g // 2)


    loads[4].wait()
    loads[5].wait()

    def gradient(c):
        span = pl.ds(pl.multiple_of(c * chunk, 128), chunk)
        acc = grad[:, span]
        for _, t in others:
            acc = acc + dot(dyn[t], jnp.maximum(pre_all[t, :, span], 0), 0, 0)
        grad[:, span] = acc
        sq = acc * acc
        rn = 0.8 * rf[0:1, span] + 0.2 * (jnp.sum(sq, axis=0, keepdims=True) / d + 1e-30)
        newrow[0:1, span] = rn
        for k, x in enumerate((sq, sq * (1.0 / rn))):
            folded = x[:, 0:128]
            for b in range(1, chunk // 128):
                folded = folded + x[:, b * 128:b * 128 + 128]
            colacc[k, 0:d, :] += folded

    with jax.named_scope("grad"):
        loop(ff // chunk, gradient)
    blocks = [(b, min(b + 128, d)) for b in range(0, d, 128)]
    for k in range(2):
        for lo, hi in blocks:
            sums = jnp.sum(colacc[k, lo:lo + 128, :].T, axis=0, keepdims=True)
            colst[i, k:k + 1, lo:hi] = sums[:, 0:hi - lo]
    for o, t in others:
        send_st(o, t).start()
    @pl.when(outer)
    def _():
        send_cross(1)

    @pl.when(inner)
    def _():
        send_cross(0, g // 2, g // 2)

    @pl.when(jnp.logical_not(inner))
    def _():
        send_cross(0)


    with jax.named_scope("waitst"):
        for o, t in others:
            pltpu.make_async_copy(colst.at[i], colst.at[t], st_r.at[o - 1]).wait()
    col, weighted = jnp.zeros((1, d), F32), jnp.zeros((1, d), F32)
    for t in range(n_dp):
        col = col + colst[t, 0:1, :]
        weighted = weighted + colst[t, 1:2, :]
    full = ff * n_dp
    cn = 0.8 * cf[...] + 0.2 * (col / full + 1e-30)
    newcol[...] = cn
    spread = jnp.sqrt(jnp.sum(weighted / cn, axis=1, keepdims=True) / (full * d))
    cspad[...] = jnp.zeros_like(cspad)
    cspad[0:1, 0:d] = lax.rsqrt(cn) / jnp.maximum(1.0, spread / 0.01)
    for lo, hi in blocks:
        cscol[lo:lo + 128, :] = jnp.broadcast_to(cspad[0:1, lo:lo + 128], (128, 128)).T

    def apply(c):
        span = pl.ds(pl.multiple_of(c * deep, 16), deep)
        update = grad[span, :] * lax.rsqrt(newrow[...]) * cscol[span, 0:1]
        neww[0, span, :] = (wv[span, :].astype(F32) - update).astype(BF16)

    with jax.named_scope("apply"):
        loop(d // deep, apply)

    for o, t in [(0, i)] + others:
        with jax.named_scope("waitret%d" % o):
            pltpu.make_async_copy(snd.at[0], ret.at[t], rt_r.at[o]).wait()

    def sent(src, sem):
        pltpu.make_async_copy(src, src, sem).wait()

    with jax.named_scope("sent"):
        sent(dy_out.at[0:n_e - 1], dy_s.at[0])
        sent(snd.at[0, 0:n_e - 1], rt_s.at[0])
        for o, t in others:
            sent(pre_all.at[0], pre_s.at[o - 1])
            sent(dyn.at[0, :, 0:main], fw_s.at[o - 1, 0])
            if last:
                sent(ends.at[0], fw_s.at[o - 1, 1])
            sent(snd.at[0], rt_s.at[o])
            sent(colst.at[0], st_s.at[o - 1])


def finish(packed, ff, ret, place, neww, newrow, newcol, hid_o, neww_o, newrow_o, newcol_o, hid, sem):
    copies = [pltpu.make_async_copy(x, y, sem.at[k]) for k, (x, y) in enumerate((
        (neww, neww_o), (newrow, newrow_o), (newcol, newcol_o)))]
    for copy in copies:
        copy.start()
    half = ff // 2
    wide = half if packed else ff
    for t in range(ret.shape[0]):
        for c in range(2 if packed else 1):
            got = dot(place[0], flat_rows(ret[t, :, :, c * wide:c * wide + wide]), 0, 0)
            if packed:
                got = got + dot(place[1 + c], flat_rows(ret[t, :, :, ff:ff + half]), 0, 0)
            hid[:, t * ff + c * wide:t * ff + c * wide + wide] = got.astype(BF16)
        span = slice(t * ff, t * ff + ff)
        copies.append(pltpu.make_async_copy(hid.at[:, span], hid_o.at[:, span], sem.at[3 + t]))
        copies[-1].start()
    for copy in copies:
        copy.wait()


def shards(out_grad, routes, pre_act, out_weight, row_factor, col_factor):
    n_dp, n_e = lax.axis_size("dp"), lax.axis_size("expert")
    tok, d = out_grad.shape
    r = pre_act.shape[0]
    ff = out_weight.shape[1]
    slot = r // n_e
    packed = slot > 8
    assert slot <= 12
    kinds = 3 if packed else 1
    assert n_e >= 4 and n_e & (n_e - 1) == 0
    g = n_e // 4
    assert g * slot <= 128
    chunk = next(c for c in (384, 256, 128) if ff % c == 0)
    deep = max(c for c in range(16, 257, 16) if d % c == 0)
    wide_d = up128(d) + d // 2 // 128 * 128 if packed else d
    assert not packed or 2 * d - d // 256 * 256 <= up128(d)
    wide_f = ff + ff // 2 if packed else ff
    vm = pl.BlockSpec(memory_space=pltpu.VMEM)
    hbm = pl.BlockSpec(memory_space=pl.ANY)
    dma = pltpu.SemaphoreType.DMA
    out = pltpu.VMEM
    held = pl.pallas_call(
        functools.partial(kernel, (n_dp, n_e, slot, chunk, deep)),
        out_shape=(out((n_dp, n_e, 8, wide_f), BF16), out((kinds, n_e * 8, tok), BF16),
                   out((1, d, ff), BF16), out((1, ff), F32), out((1, d), F32)),
        in_specs=[hbm] * 6,
        out_specs=(vm,) * 5,
        scratch_shapes=[
            pltpu.VMEM((d, tok), BF16),
            pltpu.VMEM((1, tok), jnp.int32),
            pltpu.VMEM((1, ff), F32),
            pltpu.VMEM((1, d), F32),
            pltpu.VMEM((kinds, g * slot, g * 8), BF16),
            pltpu.VMEM((kinds, g * 8, g * slot), BF16),
            pltpu.VMEM((g * slot, 128), BF16),
            pltpu.VMEM((n_dp, 4, max(d % 128, 1), 128), BF16),
            pltpu.VMEM((n_e, 8, wide_d), BF16),
            pltpu.VMEM((n_e, 8, wide_d), BF16),
            pltpu.VMEM((n_dp, r, d), BF16),
            pltpu.VMEM((n_dp, r, ff), BF16),
            pltpu.VMEM((d, ff), BF16),
            pltpu.VMEM((d, ff), F32),
            pltpu.VMEM((n_dp, n_e, 8, wide_f), BF16),
            pltpu.VMEM((n_dp, 2, d), F32),
            pltpu.VMEM((2, up128(d), 128), F32),
            pltpu.VMEM((1, up128(d)), F32),
            pltpu.VMEM((up128(d), 128), F32),
            dma((6,)), pltpu.SemaphoreType.REGULAR((n_e.bit_length() - 1,)), dma((1,)), dma((4,)),
            dma((n_dp - 1, 2)), dma((n_dp - 1, 4, 2)), dma((n_dp - 1,)), dma((n_dp - 1,)),
            dma((n_dp,)), dma((n_dp,)), dma((n_dp - 1,)), dma((n_dp - 1,)),
        ],
        compiler_params=pltpu.CompilerParams(
            collective_id=0, has_side_effects=True, vmem_limit_bytes=59 * 1024 * 1024),
    )(out_grad.T, routes.reshape(1, tok), pre_act, jnp.swapaxes(out_weight, 1, 2), row_factor,
      col_factor)
    hid, neww, newrow, newcol = pl.pallas_call(
        functools.partial(finish, packed, ff),
        out_shape=tuple(jax.ShapeDtypeStruct(*x) for x in (
            ((tok, ff * n_dp), BF16), ((1, d, ff), BF16), ((1, ff), F32), ((1, d), F32))),
        in_specs=[vm] * 5,
        out_specs=[hbm] * 4,
        scratch_shapes=[pltpu.VMEM((tok, ff * n_dp), BF16), dma((3 + n_dp,))],
        compiler_params=pltpu.CompilerParams(vmem_limit_bytes=8 * 1024 * 1024),
    )(*held)
    return hid, jnp.swapaxes(neww, 1, 2), newrow, newcol


def solution(mesh):
    placed = (
        P(("dp", "expert"), None),
        P(("dp", "expert"), None),
        P(("dp", "expert"), None),
        P("expert", "dp", None),
        P("expert", "dp"),
        P("expert", None),
    )
    return jax.shard_map(
        shards,
        mesh=mesh,
        in_specs=placed,
        out_specs=(
            P(("dp", "expert"), None),
            P("expert", "dp", None),
            P("expert", "dp"),
            P("expert", None),
        ),
        check_vma=False,
    )
```

```python
import functools
import jax
import jax.numpy as jnp
from jax import lax
from jax.experimental import pallas as pl
from jax.experimental.pallas import tpu as pltpu
from jax.sharding import PartitionSpec as P

MESH = pl.DeviceIdType.MESH
F32, BF16 = jnp.float32, jnp.bfloat16


def up128(n):
    return -(-n // 128) * 128


def dot(a, b, ca=1, cb=0):
    return lax.dot_general(a, b, (((ca,), (cb,)), ((), ())), preferred_element_type=F32)


def onehot(hit):
    return jnp.where(hit, 1.0, 0.0).astype(BF16)


def flat_rows(x):
    return x.astype(F32).reshape(x.shape[0] * 8, x.shape[2]).astype(BF16)


def kernel(cfg, og_h, rrow_h, pre, w, rf_h, cf_h,
           ret, place, neww, newrow, newcol,
           og, rrow, rf, cf, qn, qt, eye, ends,
           dy_out, dy_all, dyn, pre_all, wv, grad, snd, colst, colacc, cspad, cscol,
           loc, flood, dy_s, dy_r, fw_s, fw_r, pre_s, pre_r, rt_s, rt_r, st_s, st_r):
    n_dp, n_e, slot, chunk, deep = cfg
    d, tok = og.shape
    ff = wv.shape[1]
    packed = slot > 8
    half, dp_off, h0 = ff // 2, up128(d), d // 2 // 128 * 128
    rest = d - 2 * h0
    main, last = d // 128 * 128, d % 128
    bits = n_e.bit_length() - 1
    g = n_e // 4
    n = g * slot
    i, e = lax.axis_index("dp"), lax.axis_index("expert")
    others = [(o, lax.rem(i + o, n_dp)) for o in range(1, n_dp)]

    def flip(x, b):
        return x + (1 - 2 * lax.rem(lax.div(x, 1 << b), 2)) * (1 << b)

    def loop(count, act):
        def step(k, _):
            act(k)
            return 0
        lax.fori_loop(0, count, step, 0)

    barrier = pltpu.get_barrier_semaphore()
    for _, t in others:
        pl.semaphore_signal(barrier, inc=1, device_id=(t, e), device_id_type=MESH)
    for b in range(bits):
        pl.semaphore_signal(barrier, inc=1, device_id=(i, flip(e, b)), device_id_type=MESH)

    cols = lambda t: pl.ds(pl.multiple_of(t * ff, 128), ff)
    loads = [pltpu.make_async_copy(x, y, loc.at[k]) for k, (x, y) in enumerate((
        (rrow_h, rrow), (og_h, og), (w.at[0], wv), (pre.at[:, cols(i)], pre_all.at[i]), (rf_h, rf),
        (cf_h, cf)))]
    for load in loads:
        load.start()

    def tables(q, rows, cells, axis):
        for k in range(q.shape[0]):
            row = lax.broadcasted_iota(jnp.int32, (rows, cells), axis)
            cell = lax.broadcasted_iota(jnp.int32, (rows, cells), 1 - axis)
            at = cell & 7
            wants = slot * (cell >> 3) + at + (0, 8, 4)[k]
            held = (at < min(slot, 8), at < slot - 8, at >= 4)[k]
            q[k] = onehot((row == wants) & held)

    tables(qn, n, g * 8, 0)
    tables(qt, g * 8, n, 1)
    if last:
        eye[...] = onehot(lax.broadcasted_iota(jnp.int32, (n, 128), 0)
                          == lax.broadcasted_iota(jnp.int32, (n, 128), 1))

    loads[0].wait()
    named = jnp.broadcast_to(rrow[...].astype(F32), (tok, tok))
    same = named == named.T
    at_row = lax.broadcasted_iota(jnp.int32, (tok, tok), 0)
    at_col = lax.broadcasted_iota(jnp.int32, (tok, tok), 1)
    order = jnp.sum(jnp.where(same & (at_row < at_col), 1.0, 0.0), axis=0, keepdims=True)
    base = rrow[...].astype(F32) * 8.0 + order
    rows = lax.broadcasted_iota(jnp.int32, (n_e * 8, tok), 0).astype(F32)
    place[0] = onehot(rows == jnp.where(order < 8.0, base, -1.0))
    if packed:
        place[1] = onehot(rows == jnp.where(order >= 8.0, base - 8.0, -1.0))
        place[2] = onehot(rows == jnp.where(order >= 8.0, base - 4.0, -1.0))
    loads[1].wait()
    dy_out[:, :, 0:d] = dot(place[0], og[...], 1, 1).reshape(n_e, 8, d).astype(BF16)
    if packed:
        tail = dot(place[1], og[0:h0, :], 1, 1) + dot(place[2], og[h0:2 * h0, :], 1, 1)
        dy_out[:, :, dp_off:dp_off + h0] = tail.reshape(n_e, 8, h0).astype(BF16)
        if rest:
            more = dot(place[1], og[2 * h0:d, :], 1, 1)
            dy_out[:, :, d:d + rest] = more.reshape(n_e, 8, rest).astype(BF16)

    quarter = lax.div(e, g)
    inner = lax.rem(quarter + 1, 4) >= 2
    outer = lax.rem(quarter + 1, 4) < 2
    group = {0: quarter, 1: flip(quarter, 0), 2: flip(quarter, 1), 3: flip(flip(quarter, 0), 1)}

    def members(k, act):
        if k:
            loop(g, lambda m: act(group[k] * g + m))
        else:
            loop(g - 1, lambda m: act(quarter * g + lax.rem(e + 1 + m, g)))

    def send_dy(k, t):
        return pltpu.make_async_remote_copy(
            src_ref=dy_out.at[t], dst_ref=dy_all.at[e], send_sem=dy_s.at[0],
            recv_sem=dy_r.at[k], device_id=(i, t), device_id_type=MESH)

    def rows_of(k):
        return pl.ds(pl.multiple_of(group[k] * n, 16), n)

    def send_pre(o, t):
        return pltpu.make_async_remote_copy(
            src_ref=pre.at[:, cols(t)], dst_ref=pre_all.at[i],
            send_sem=pre_s.at[o - 1], recv_sem=pre_r.at[n_dp - o - 1], device_id=(t, e),
            device_id_type=MESH)

    def send_fw(o, t, k):
        refs = [dyn.at[i, rows_of(k), 0:main]] + ([ends.at[i, group[k]]] if last else [])
        return [pltpu.make_async_remote_copy(
            src_ref=x, dst_ref=x, send_sem=fw_s.at[o - 1, m], recv_sem=fw_r.at[n_dp - o - 1, k, m],
            device_id=(t, e), device_id_type=MESH) for m, x in enumerate(refs)]

    def send_ret(o, t, j):
        return pltpu.make_async_remote_copy(
            src_ref=snd.at[t, j], dst_ref=ret.at[i, e], send_sem=rt_s.at[o],
            recv_sem=rt_r.at[lax.rem(n_dp - o, n_dp)], device_id=(t, j), device_id_type=MESH)

    def send_st(o, t):
        return pltpu.make_async_remote_copy(
            src_ref=colst.at[i], dst_ref=colst.at[i], send_sem=st_s.at[o - 1],
            recv_sem=st_r.at[n_dp - o - 1], device_id=(t, e), device_id_type=MESH)

    def meet(b):
        pl.semaphore_signal(flood.at[b], inc=1, device_id=(i, flip(e, b)), device_id_type=MESH)
        pl.semaphore_wait(flood.at[b], 1)

    with jax.named_scope("bar"):
        pl.semaphore_wait(barrier, bits + n_dp - 1)
    for o, t in others:
        send_pre(o, t).start()
    across = flip(e, bits - 1)
    send_dy(2, across).start()
    with jax.named_scope("flood"):
        for b in range(bits - 2):
            meet(b)
            first = lax.div(flip(across, b), 1 << b) * (1 << b)
            loop(1 << b, lambda m: send_dy(2, first + m).start())
    with jax.named_scope("flood2"):
        meet(bits - 2)
    for k in (3, 1, 0):
        members(k, lambda t: send_dy(k, t).start())
    own = pltpu.make_async_copy(dy_out.at[e], dy_all.at[e], dy_r.at[0])
    own.start()

    colacc[...] = jnp.zeros_like(colacc)

    def unpack(k):
        part = pl.ds(group[k] * g, g)
        dy = dot(qn[0], flat_rows(dy_all[part, :, 0:d]))
        if packed:
            q_lo, q_hi = qn[1], qn[2]
            tail = flat_rows(dy_all[part, :, dp_off:dp_off + h0])
            pieces = [dot(q_lo, tail), dot(q_hi, tail)]
            if rest:
                more = dot(q_lo, flat_rows(dy_all[part, :, 2 * h0:dp_off]))
                pieces.append(more[:, d - 2 * h0:d - 2 * h0 + rest])
            dy = dy + jnp.concatenate(pieces, axis=1)
        dy = dy.astype(BF16)
        dyn[i, rows_of(k), :] = dy
        if last:
            ends[i, group[k]] = dot(dy[:, main:d], eye[...], 0, 0).astype(BF16)
        return dy

    def back(t, k, dy):
        part = pl.ds(group[k] * g, g)
        where = rows_of(k)
        tail = None
        for c in range(2 if packed else 1):
            wide = half if packed else ff
            span = slice(c * wide, c * wide + wide)
            bk = dot(dy, wv[:, span])
            keep = pre_all[t, where, span].astype(F32) > 0.0
            bk = jnp.where(keep, bk, 0.0).astype(BF16)
            snd[t, part, :, span] = dot(qt[0], bk).reshape(g, 8, wide).astype(BF16)
            if packed:
                more = dot(qt[1 + c], bk)
                tail = more if tail is None else tail + more
        if packed:
            snd[t, part, :, ff:ff + half] = tail.reshape(g, 8, half).astype(BF16)

    def arrive(k):
        part = pl.ds(group[k] * g, g)
        with jax.named_scope("recv%d" % k):
            pltpu.make_async_copy(dy_out.at[part], dy_all.at[part], dy_r.at[k]).wait()

    def forward(k):
        for o, t in others:
            for copy in send_fw(o, t, k):
                copy.start()

    def near(k):
        with jax.named_scope("back%d" % k):
            back(i, k, unpack(k))
        members(k, lambda j: send_ret(0, i, j).start())

    def await_cross(k):
        for o, t in others:
            with jax.named_scope("waitfw%d" % k):
                rows = dyn.at[t, rows_of(k), 0:main]
                pltpu.make_async_copy(rows, rows, fw_r.at[o - 1, k, 0]).wait()
                if last:
                    tile = ends.at[t, group[k]]
                    pltpu.make_async_copy(tile, tile, fw_r.at[o - 1, k, 1]).wait()
                    dyn[t, rows_of(k), main:d] = dot(eye[...], ends[t, group[k]], 1, 1).astype(BF16)

    def back_cross(k):
        for _, t in others:
            with jax.named_scope("backx%d" % k):
                back(t, k, dyn[t, rows_of(k), :])

    def cross(k):
        await_cross(k)
        back_cross(k)

    def send_cross(k, first=0, count=g):
        for o, t in others:
            loop(count, lambda m: send_ret(o, t, group[k] * g + first + m).start())

    arrive(2)
    loads[2].wait()
    loads[3].wait()
    near(2)
    forward(2)
    arrive(3)
    near(3)
    forward(3)
    arrive(1)
    near(1)
    forward(1)
    arrive(0)
    near(0)
    forward(0)
    own_ret = pltpu.make_async_copy(snd.at[i, e], ret.at[i, e], rt_r.at[0])
    own_ret.start()
    for o, t in others:
        pltpu.make_async_copy(pre_all.at[i], pre_all.at[t], pre_r.at[o - 1]).wait()
    cross(2)
    def gradient_own(c):
        span = pl.ds(pl.multiple_of(c * chunk, 128), chunk)
        grad[:, span] = dot(dyn[i], jnp.maximum(pre_all[i, :, span], 0), 0, 0)

    with jax.named_scope("gradown"):
        loop(ff // chunk, gradient_own)
    cross(3)
    cross(1)
    send_cross(2)
    send_cross(3)
    await_cross(0)
    @pl.when(inner)
    def _():
        send_cross(1)

    back_cross(0)
    @pl.when(inner)
    def _():
        send_cross(0, 0, g // 2)


    loads[4].wait()
    loads[5].wait()

    def gradient(c):
        span = pl.ds(pl.multiple_of(c * chunk, 128), chunk)
        acc = grad[:, span]
        for _, t in others:
            acc = acc + dot(dyn[t], jnp.maximum(pre_all[t, :, span], 0), 0, 0)
        grad[:, span] = acc
        sq = acc * acc
        rn = 0.8 * rf[0:1, span] + 0.2 * (jnp.sum(sq, axis=0, keepdims=True) / d + 1e-30)
        newrow[0:1, span] = rn
        for k, x in enumerate((sq, sq * (1.0 / rn))):
            folded = x[:, 0:128]
            for b in range(1, chunk // 128):
                folded = folded + x[:, b * 128:b * 128 + 128]
            colacc[k, 0:d, :] += folded

    with jax.named_scope("grad"):
        loop(ff // chunk, gradient)
    blocks = [(b, min(b + 128, d)) for b in range(0, d, 128)]
    for k in range(2):
        for lo, hi in blocks:
            sums = jnp.sum(colacc[k, lo:lo + 128, :].T, axis=0, keepdims=True)
            colst[i, k:k + 1, lo:hi] = sums[:, 0:hi - lo]
    for o, t in others:
        send_st(o, t).start()
    @pl.when(outer)
    def _():
        send_cross(1)

    @pl.when(inner)
    def _():
        send_cross(0, g // 2, g // 2)

    @pl.when(jnp.logical_not(inner))
    def _():
        send_cross(0)


    with jax.named_scope("waitst"):
        for o, t in others:
            pltpu.make_async_copy(colst.at[i], colst.at[t], st_r.at[o - 1]).wait()
    col, weighted = jnp.zeros((1, d), F32), jnp.zeros((1, d), F32)
    for t in range(n_dp):
        col = col + colst[t, 0:1, :]
        weighted = weighted + colst[t, 1:2, :]
    full = ff * n_dp
    cn = 0.8 * cf[...] + 0.2 * (col / full + 1e-30)
    newcol[...] = cn
    spread = jnp.sqrt(jnp.sum(weighted / cn, axis=1, keepdims=True) / (full * d))
    cspad[...] = jnp.zeros_like(cspad)
    cspad[0:1, 0:d] = lax.rsqrt(cn) / jnp.maximum(1.0, spread / 0.01)
    for lo, hi in blocks:
        cscol[lo:lo + 128, :] = jnp.broadcast_to(cspad[0:1, lo:lo + 128], (128, 128)).T

    def apply(c):
        span = pl.ds(pl.multiple_of(c * deep, 16), deep)
        update = grad[span, :] * lax.rsqrt(newrow[...]) * cscol[span, 0:1]
        neww[0, span, :] = (wv[span, :].astype(F32) - update).astype(BF16)

    with jax.named_scope("apply"):
        loop(d // deep, apply)

    for o, t in [(0, i)] + others:
        with jax.named_scope("waitret%d" % o):
            pltpu.make_async_copy(snd.at[0], ret.at[t], rt_r.at[o]).wait()

    def sent(src, sem):
        pltpu.make_async_copy(src, src, sem).wait()

    with jax.named_scope("sent"):
        sent(dy_out.at[0:n_e - 1], dy_s.at[0])
        sent(snd.at[0, 0:n_e - 1], rt_s.at[0])
        for o, t in others:
            sent(pre_all.at[0], pre_s.at[o - 1])
            sent(dyn.at[0, :, 0:main], fw_s.at[o - 1, 0])
            if last:
                sent(ends.at[0], fw_s.at[o - 1, 1])
            sent(snd.at[0], rt_s.at[o])
            sent(colst.at[0], st_s.at[o - 1])


def finish(packed, ff, ret, place, neww, newrow, newcol, hid_o, neww_o, newrow_o, newcol_o, hid, sem):
    copies = [pltpu.make_async_copy(x, y, sem.at[k]) for k, (x, y) in enumerate((
        (neww, neww_o), (newrow, newrow_o), (newcol, newcol_o)))]
    for copy in copies:
        copy.start()
    half = ff // 2
    wide = half if packed else ff
    for t in range(ret.shape[0]):
        for c in range(2 if packed else 1):
            got = dot(place[0], flat_rows(ret[t, :, :, c * wide:c * wide + wide]), 0, 0)
            if packed:
                got = got + dot(place[1 + c], flat_rows(ret[t, :, :, ff:ff + half]), 0, 0)
            hid[:, t * ff + c * wide:t * ff + c * wide + wide] = got.astype(BF16)
        span = slice(t * ff, t * ff + ff)
        copies.append(pltpu.make_async_copy(hid.at[:, span], hid_o.at[:, span], sem.at[3 + t]))
        copies[-1].start()
    for copy in copies:
        copy.wait()


def shards(out_grad, routes, pre_act, out_weight, row_factor, col_factor):
    n_dp, n_e = lax.axis_size("dp"), lax.axis_size("expert")
    tok, d = out_grad.shape
    r = pre_act.shape[0]
    ff = out_weight.shape[1]
    slot = r // n_e
    packed = slot > 8
    assert slot <= 12
    kinds = 3 if packed else 1
    assert n_e >= 4 and n_e & (n_e - 1) == 0
    g = n_e // 4
    assert g * slot <= 128
    chunk = next(c for c in (384, 256, 128) if ff % c == 0)
    deep = max(c for c in range(16, 257, 16) if d % c == 0)
    wide_d = up128(d) + d // 2 // 128 * 128 if packed else d
    assert not packed or 2 * d - d // 256 * 256 <= up128(d)
    wide_f = ff + ff // 2 if packed else ff
    vm = pl.BlockSpec(memory_space=pltpu.VMEM)
    hbm = pl.BlockSpec(memory_space=pl.ANY)
    dma = pltpu.SemaphoreType.DMA
    out = pltpu.VMEM
    held = pl.pallas_call(
        functools.partial(kernel, (n_dp, n_e, slot, chunk, deep)),
        out_shape=(out((n_dp, n_e, 8, wide_f), BF16), out((kinds, n_e * 8, tok), BF16),
                   out((1, d, ff), BF16), out((1, ff), F32), out((1, d), F32)),
        in_specs=[hbm] * 6,
        out_specs=(vm,) * 5,
        scratch_shapes=[
            pltpu.VMEM((d, tok), BF16),
            pltpu.VMEM((1, tok), jnp.int32),
            pltpu.VMEM((1, ff), F32),
            pltpu.VMEM((1, d), F32),
            pltpu.VMEM((kinds, g * slot, g * 8), BF16),
            pltpu.VMEM((kinds, g * 8, g * slot), BF16),
            pltpu.VMEM((g * slot, 128), BF16),
            pltpu.VMEM((n_dp, 4, max(d % 128, 1), 128), BF16),
            pltpu.VMEM((n_e, 8, wide_d), BF16),
            pltpu.VMEM((n_e, 8, wide_d), BF16),
            pltpu.VMEM((n_dp, r, d), BF16),
            pltpu.VMEM((n_dp, r, ff), BF16),
            pltpu.VMEM((d, ff), BF16),
            pltpu.VMEM((d, ff), F32),
            pltpu.VMEM((n_dp, n_e, 8, wide_f), BF16),
            pltpu.VMEM((n_dp, 2, d), F32),
            pltpu.VMEM((2, up128(d), 128), F32),
            pltpu.VMEM((1, up128(d)), F32),
            pltpu.VMEM((up128(d), 128), F32),
            dma((6,)), pltpu.SemaphoreType.REGULAR((n_e.bit_length() - 1,)), dma((1,)), dma((4,)),
            dma((n_dp - 1, 2)), dma((n_dp - 1, 4, 2)), dma((n_dp - 1,)), dma((n_dp - 1,)),
            dma((n_dp,)), dma((n_dp,)), dma((n_dp - 1,)), dma((n_dp - 1,)),
        ],
        compiler_params=pltpu.CompilerParams(
            collective_id=0, has_side_effects=True, vmem_limit_bytes=59 * 1024 * 1024),
    )(out_grad.T, routes.reshape(1, tok), pre_act, jnp.swapaxes(out_weight, 1, 2), row_factor,
      col_factor)
    hid, neww, newrow, newcol = pl.pallas_call(
        functools.partial(finish, packed, ff),
        out_shape=tuple(jax.ShapeDtypeStruct(*x) for x in (
            ((tok, ff * n_dp), BF16), ((1, d, ff), BF16), ((1, ff), F32), ((1, d), F32))),
        in_specs=[vm] * 5,
        out_specs=[hbm] * 4,
        scratch_shapes=[pltpu.VMEM((tok, ff * n_dp), BF16), dma((3 + n_dp,))],
        compiler_params=pltpu.CompilerParams(vmem_limit_bytes=8 * 1024 * 1024),
    )(*held)
    return hid, jnp.swapaxes(neww, 1, 2), newrow, newcol


def solution(mesh):
    placed = (
        P(("dp", "expert"), None),
        P(("dp", "expert"), None),
        P(("dp", "expert"), None),
        P("expert", "dp", None),
        P("expert", "dp"),
        P("expert", None),
    )
    return jax.shard_map(
        shards,
        mesh=mesh,
        in_specs=placed,
        out_specs=(
            P(("dp", "expert"), None),
            P("expert", "dp", None),
            P("expert", "dp"),
            P("expert", None),
        ),
        check_vma=False,
    )
```

```python
import functools
import jax
import jax.numpy as jnp
from jax import lax
from jax.experimental import pallas as pl
from jax.experimental.pallas import tpu as pltpu
from jax.sharding import PartitionSpec as P

MESH = pl.DeviceIdType.MESH
F32, BF16 = jnp.float32, jnp.bfloat16


def up128(n):
    return -(-n // 128) * 128


def dot(a, b, ca=1, cb=0):
    return lax.dot_general(a, b, (((ca,), (cb,)), ((), ())), preferred_element_type=F32)


def onehot(hit):
    return jnp.where(hit, 1.0, 0.0).astype(BF16)


def flat_rows(x):
    return x.astype(F32).reshape(x.shape[0] * 8, x.shape[2]).astype(BF16)


def kernel(cfg, og_h, rrow_h, pre, w, rf_h, cf_h,
           ret, place, neww, newrow, newcol,
           og, rrow, rf, cf, qn, qt, eye, ends,
           dy_out, dy_all, dyn, pre_all, wv, grad, snd, colst, colacc, cspad, cscol,
           loc, flood, dy_s, dy_r, fw_s, fw_r, pre_s, pre_r, rt_s, rt_r, st_s, st_r):
    n_dp, n_e, slot, chunk, deep = cfg
    d, tok = og.shape
    ff = wv.shape[1]
    packed = slot > 8
    half, dp_off, h0 = ff // 2, up128(d), d // 2 // 128 * 128
    rest = d - 2 * h0
    main, last = d // 128 * 128, d % 128
    bits = n_e.bit_length() - 1
    g = n_e // 4
    n = g * slot
    i, e = lax.axis_index("dp"), lax.axis_index("expert")
    others = [(o, lax.rem(i + o, n_dp)) for o in range(1, n_dp)]

    def flip(x, b):
        return x + (1 - 2 * lax.rem(lax.div(x, 1 << b), 2)) * (1 << b)

    def loop(count, act):
        def step(k, _):
            act(k)
            return 0
        lax.fori_loop(0, count, step, 0)

    barrier = pltpu.get_barrier_semaphore()
    for _, t in others:
        pl.semaphore_signal(barrier, inc=1, device_id=(t, e), device_id_type=MESH)
    for b in range(bits):
        pl.semaphore_signal(barrier, inc=1, device_id=(i, flip(e, b)), device_id_type=MESH)

    cols = lambda t: pl.ds(pl.multiple_of(t * ff, 128), ff)
    loads = [pltpu.make_async_copy(x, y, loc.at[k]) for k, (x, y) in enumerate((
        (rrow_h, rrow), (og_h, og), (w.at[0], wv), (pre.at[:, cols(i)], pre_all.at[i]), (rf_h, rf),
        (cf_h, cf)))]
    for load in loads:
        load.start()

    def tables(q, rows, cells, axis):
        for k in range(q.shape[0]):
            row = lax.broadcasted_iota(jnp.int32, (rows, cells), axis)
            cell = lax.broadcasted_iota(jnp.int32, (rows, cells), 1 - axis)
            at = cell & 7
            wants = slot * (cell >> 3) + at + (0, 8, 4)[k]
            held = (at < min(slot, 8), at < slot - 8, at >= 4)[k]
            q[k] = onehot((row == wants) & held)

    tables(qn, n, g * 8, 0)
    tables(qt, g * 8, n, 1)
    if last:
        eye[...] = onehot(lax.broadcasted_iota(jnp.int32, (n, 128), 0)
                          == lax.broadcasted_iota(jnp.int32, (n, 128), 1))

    loads[0].wait()
    named = jnp.broadcast_to(rrow[...].astype(F32), (tok, tok))
    same = named == named.T
    at_row = lax.broadcasted_iota(jnp.int32, (tok, tok), 0)
    at_col = lax.broadcasted_iota(jnp.int32, (tok, tok), 1)
    order = jnp.sum(jnp.where(same & (at_row < at_col), 1.0, 0.0), axis=0, keepdims=True)
    base = rrow[...].astype(F32) * 8.0 + order
    rows = lax.broadcasted_iota(jnp.int32, (n_e * 8, tok), 0).astype(F32)
    place[0] = onehot(rows == jnp.where(order < 8.0, base, -1.0))
    if packed:
        place[1] = onehot(rows == jnp.where(order >= 8.0, base - 8.0, -1.0))
        place[2] = onehot(rows == jnp.where(order >= 8.0, base - 4.0, -1.0))
    loads[1].wait()
    dy_out[:, :, 0:d] = dot(place[0], og[...], 1, 1).reshape(n_e, 8, d).astype(BF16)
    if packed:
        tail = dot(place[1], og[0:h0, :], 1, 1) + dot(place[2], og[h0:2 * h0, :], 1, 1)
        dy_out[:, :, dp_off:dp_off + h0] = tail.reshape(n_e, 8, h0).astype(BF16)
        if rest:
            more = dot(place[1], og[2 * h0:d, :], 1, 1)
            dy_out[:, :, d:d + rest] = more.reshape(n_e, 8, rest).astype(BF16)

    quarter = lax.div(e, g)
    inner = lax.rem(quarter + 1, 4) >= 2
    outer = lax.rem(quarter + 1, 4) < 2
    group = {0: quarter, 1: flip(quarter, 0), 2: flip(quarter, 1), 3: flip(flip(quarter, 0), 1)}

    def members(k, act):
        if k:
            loop(g, lambda m: act(group[k] * g + m))
        else:
            loop(g - 1, lambda m: act(quarter * g + lax.rem(e + 1 + m, g)))

    def send_dy(k, t):
        return pltpu.make_async_remote_copy(
            src_ref=dy_out.at[t], dst_ref=dy_all.at[e], send_sem=dy_s.at[0],
            recv_sem=dy_r.at[k], device_id=(i, t), device_id_type=MESH)

    def rows_of(k):
        return pl.ds(pl.multiple_of(group[k] * n, 16), n)

    def send_pre(o, t):
        return pltpu.make_async_remote_copy(
            src_ref=pre.at[:, cols(t)], dst_ref=pre_all.at[i],
            send_sem=pre_s.at[o - 1], recv_sem=pre_r.at[n_dp - o - 1], device_id=(t, e),
            device_id_type=MESH)

    def send_fw(o, t, k):
        refs = [dyn.at[i, rows_of(k), 0:main]] + ([ends.at[i, group[k]]] if last else [])
        return [pltpu.make_async_remote_copy(
            src_ref=x, dst_ref=x, send_sem=fw_s.at[o - 1, m], recv_sem=fw_r.at[n_dp - o - 1, k, m],
            device_id=(t, e), device_id_type=MESH) for m, x in enumerate(refs)]

    def send_ret(o, t, j):
        return pltpu.make_async_remote_copy(
            src_ref=snd.at[t, j], dst_ref=ret.at[i, e], send_sem=rt_s.at[o],
            recv_sem=rt_r.at[lax.rem(n_dp - o, n_dp)], device_id=(t, j), device_id_type=MESH)

    def send_st(o, t):
        return pltpu.make_async_remote_copy(
            src_ref=colst.at[i], dst_ref=colst.at[i], send_sem=st_s.at[o - 1],
            recv_sem=st_r.at[n_dp - o - 1], device_id=(t, e), device_id_type=MESH)

    def meet(b):
        pl.semaphore_signal(flood.at[b], inc=1, device_id=(i, flip(e, b)), device_id_type=MESH)
        pl.semaphore_wait(flood.at[b], 1)

    with jax.named_scope("bar"):
        pl.semaphore_wait(barrier, bits + n_dp - 1)
    for o, t in others:
        send_pre(o, t).start()
    across = flip(e, bits - 1)
    send_dy(2, across).start()
    with jax.named_scope("flood"):
        for b in range(bits - 2):
            meet(b)
            first = lax.div(flip(across, b), 1 << b) * (1 << b)
            loop(1 << b, lambda m: send_dy(2, first + m).start())
    with jax.named_scope("flood2"):
        meet(bits - 2)
    for k in (3, 1, 0):
        members(k, lambda t: send_dy(k, t).start())
    own = pltpu.make_async_copy(dy_out.at[e], dy_all.at[e], dy_r.at[0])
    own.start()

    colacc[...] = jnp.zeros_like(colacc)

    def unpack(k):
        part = pl.ds(group[k] * g, g)
        dy = dot(qn[0], flat_rows(dy_all[part, :, 0:d]))
        if packed:
            q_lo, q_hi = qn[1], qn[2]
            tail = flat_rows(dy_all[part, :, dp_off:dp_off + h0])
            pieces = [dot(q_lo, tail), dot(q_hi, tail)]
            if rest:
                more = dot(q_lo, flat_rows(dy_all[part, :, 2 * h0:dp_off]))
                pieces.append(more[:, d - 2 * h0:d - 2 * h0 + rest])
            dy = dy + jnp.concatenate(pieces, axis=1)
        dy = dy.astype(BF16)
        dyn[i, rows_of(k), :] = dy
        if last:
            ends[i, group[k]] = dot(dy[:, main:d], eye[...], 0, 0).astype(BF16)
        return dy

    def back(t, k, dy):
        part = pl.ds(group[k] * g, g)
        where = rows_of(k)
        tail = None
        for c in range(2 if packed else 1):
            wide = half if packed else ff
            span = slice(c * wide, c * wide + wide)
            bk = dot(dy, wv[:, span])
            keep = pre_all[t, where, span].astype(F32) > 0.0
            bk = jnp.where(keep, bk, 0.0).astype(BF16)
            snd[t, part, :, span] = dot(qt[0], bk).reshape(g, 8, wide).astype(BF16)
            if packed:
                more = dot(qt[1 + c], bk)
                tail = more if tail is None else tail + more
        if packed:
            snd[t, part, :, ff:ff + half] = tail.reshape(g, 8, half).astype(BF16)

    def arrive(k):
        part = pl.ds(group[k] * g, g)
        with jax.named_scope("recv%d" % k):
            pltpu.make_async_copy(dy_out.at[part], dy_all.at[part], dy_r.at[k]).wait()

    def forward(k):
        for o, t in others:
            for copy in send_fw(o, t, k):
                copy.start()

    def near(k):
        with jax.named_scope("back%d" % k):
            back(i, k, unpack(k))
        members(k, lambda j: send_ret(0, i, j).start())

    def await_cross(k):
        for o, t in others:
            with jax.named_scope("waitfw%d" % k):
                rows = dyn.at[t, rows_of(k), 0:main]
                pltpu.make_async_copy(rows, rows, fw_r.at[o - 1, k, 0]).wait()
                if last:
                    tile = ends.at[t, group[k]]
                    pltpu.make_async_copy(tile, tile, fw_r.at[o - 1, k, 1]).wait()
                    dyn[t, rows_of(k), main:d] = dot(eye[...], ends[t, group[k]], 1, 1).astype(BF16)

    def back_cross(k):
        for _, t in others:
            with jax.named_scope("backx%d" % k):
                back(t, k, dyn[t, rows_of(k), :])

    def cross(k):
        await_cross(k)
        back_cross(k)

    def send_cross(k, first=0, count=g):
        for o, t in others:
            loop(count, lambda m: send_ret(o, t, group[k] * g + first + m).start())

    arrive(2)
    loads[2].wait()
    loads[3].wait()
    near(2)
    forward(2)
    arrive(3)
    near(3)
    forward(3)
    arrive(1)
    near(1)
    forward(1)
    arrive(0)
    near(0)
    forward(0)
    own_ret = pltpu.make_async_copy(snd.at[i, e], ret.at[i, e], rt_r.at[0])
    own_ret.start()
    for o, t in others:
        pltpu.make_async_copy(pre_all.at[i], pre_all.at[t], pre_r.at[o - 1]).wait()
    cross(2)
    def gradient_own(c):
        span = pl.ds(pl.multiple_of(c * chunk, 128), chunk)
        grad[:, span] = dot(dyn[i], jnp.maximum(pre_all[i, :, span], 0), 0, 0)

    with jax.named_scope("gradown"):
        loop(ff // chunk, gradient_own)
    cross(3)
    cross(1)
    send_cross(2)
    send_cross(3)
    await_cross(0)
    @pl.when(inner)
    def _():
        send_cross(1)

    back_cross(0)
    @pl.when(inner)
    def _():
        send_cross(0, 0, 3 * g // 4)


    loads[4].wait()
    loads[5].wait()

    def gradient(c):
        span = pl.ds(pl.multiple_of(c * chunk, 128), chunk)
        acc = grad[:, span]
        for _, t in others:
            acc = acc + dot(dyn[t], jnp.maximum(pre_all[t, :, span], 0), 0, 0)
        grad[:, span] = acc
        sq = acc * acc
        rn = 0.8 * rf[0:1, span] + 0.2 * (jnp.sum(sq, axis=0, keepdims=True) / d + 1e-30)
        newrow[0:1, span] = rn
        for k, x in enumerate((sq, sq * (1.0 / rn))):
            folded = x[:, 0:128]
            for b in range(1, chunk // 128):
                folded = folded + x[:, b * 128:b * 128 + 128]
            colacc[k, 0:d, :] += folded

    with jax.named_scope("grad"):
        loop(ff // chunk, gradient)
    blocks = [(b, min(b + 128, d)) for b in range(0, d, 128)]
    for k in range(2):
        for lo, hi in blocks:
            sums = jnp.sum(colacc[k, lo:lo + 128, :].T, axis=0, keepdims=True)
            colst[i, k:k + 1, lo:hi] = sums[:, 0:hi - lo]
    for o, t in others:
        send_st(o, t).start()
    @pl.when(outer)
    def _():
        send_cross(1)

    @pl.when(inner)
    def _():
        send_cross(0, 3 * g // 4, g - 3 * g // 4)

    @pl.when(jnp.logical_not(inner))
    def _():
        send_cross(0)


    with jax.named_scope("waitst"):
        for o, t in others:
            pltpu.make_async_copy(colst.at[i], colst.at[t], st_r.at[o - 1]).wait()
    col, weighted = jnp.zeros((1, d), F32), jnp.zeros((1, d), F32)
    for t in range(n_dp):
        col = col + colst[t, 0:1, :]
        weighted = weighted + colst[t, 1:2, :]
    full = ff * n_dp
    cn = 0.8 * cf[...] + 0.2 * (col / full + 1e-30)
    newcol[...] = cn
    spread = jnp.sqrt(jnp.sum(weighted / cn, axis=1, keepdims=True) / (full * d))
    cspad[...] = jnp.zeros_like(cspad)
    cspad[0:1, 0:d] = lax.rsqrt(cn) / jnp.maximum(1.0, spread / 0.01)
    for lo, hi in blocks:
        cscol[lo:lo + 128, :] = jnp.broadcast_to(cspad[0:1, lo:lo + 128], (128, 128)).T

    def apply(c):
        span = pl.ds(pl.multiple_of(c * deep, 16), deep)
        update = grad[span, :] * lax.rsqrt(newrow[...]) * cscol[span, 0:1]
        neww[0, span, :] = (wv[span, :].astype(F32) - update).astype(BF16)

    with jax.named_scope("apply"):
        loop(d // deep, apply)

    for o, t in [(0, i)] + others:
        with jax.named_scope("waitret%d" % o):
            pltpu.make_async_copy(snd.at[0], ret.at[t], rt_r.at[o]).wait()

    def sent(src, sem):
        pltpu.make_async_copy(src, src, sem).wait()

    with jax.named_scope("sent"):
        sent(dy_out.at[0:n_e - 1], dy_s.at[0])
        sent(snd.at[0, 0:n_e - 1], rt_s.at[0])
        for o, t in others:
            sent(pre_all.at[0], pre_s.at[o - 1])
            sent(dyn.at[0, :, 0:main], fw_s.at[o - 1, 0])
            if last:
                sent(ends.at[0], fw_s.at[o - 1, 1])
            sent(snd.at[0], rt_s.at[o])
            sent(colst.at[0], st_s.at[o - 1])


def finish(packed, ff, ret, place, neww, newrow, newcol, hid_o, neww_o, newrow_o, newcol_o, hid, sem):
    copies = [pltpu.make_async_copy(x, y, sem.at[k]) for k, (x, y) in enumerate((
        (neww, neww_o), (newrow, newrow_o), (newcol, newcol_o)))]
    for copy in copies:
        copy.start()
    half = ff // 2
    wide = half if packed else ff
    for t in range(ret.shape[0]):
        for c in range(2 if packed else 1):
            got = dot(place[0], flat_rows(ret[t, :, :, c * wide:c * wide + wide]), 0, 0)
            if packed:
                got = got + dot(place[1 + c], flat_rows(ret[t, :, :, ff:ff + half]), 0, 0)
            hid[:, t * ff + c * wide:t * ff + c * wide + wide] = got.astype(BF16)
        span = slice(t * ff, t * ff + ff)
        copies.append(pltpu.make_async_copy(hid.at[:, span], hid_o.at[:, span], sem.at[3 + t]))
        copies[-1].start()
    for copy in copies:
        copy.wait()


def shards(out_grad, routes, pre_act, out_weight, row_factor, col_factor):
    n_dp, n_e = lax.axis_size("dp"), lax.axis_size("expert")
    tok, d = out_grad.shape
    r = pre_act.shape[0]
    ff = out_weight.shape[1]
    slot = r // n_e
    packed = slot > 8
    assert slot <= 12
    kinds = 3 if packed else 1
    assert n_e >= 4 and n_e & (n_e - 1) == 0
    g = n_e // 4
    assert g * slot <= 128
    chunk = next(c for c in (384, 256, 128) if ff % c == 0)
    deep = max(c for c in range(16, 257, 16) if d % c == 0)
    wide_d = up128(d) + d // 2 // 128 * 128 if packed else d
    assert not packed or 2 * d - d // 256 * 256 <= up128(d)
    wide_f = ff + ff // 2 if packed else ff
    vm = pl.BlockSpec(memory_space=pltpu.VMEM)
    hbm = pl.BlockSpec(memory_space=pl.ANY)
    dma = pltpu.SemaphoreType.DMA
    out = pltpu.VMEM
    held = pl.pallas_call(
        functools.partial(kernel, (n_dp, n_e, slot, chunk, deep)),
        out_shape=(out((n_dp, n_e, 8, wide_f), BF16), out((kinds, n_e * 8, tok), BF16),
                   out((1, d, ff), BF16), out((1, ff), F32), out((1, d), F32)),
        in_specs=[hbm] * 6,
        out_specs=(vm,) * 5,
        scratch_shapes=[
            pltpu.VMEM((d, tok), BF16),
            pltpu.VMEM((1, tok), jnp.int32),
            pltpu.VMEM((1, ff), F32),
            pltpu.VMEM((1, d), F32),
            pltpu.VMEM((kinds, g * slot, g * 8), BF16),
            pltpu.VMEM((kinds, g * 8, g * slot), BF16),
            pltpu.VMEM((g * slot, 128), BF16),
            pltpu.VMEM((n_dp, 4, max(d % 128, 1), 128), BF16),
            pltpu.VMEM((n_e, 8, wide_d), BF16),
            pltpu.VMEM((n_e, 8, wide_d), BF16),
            pltpu.VMEM((n_dp, r, d), BF16),
            pltpu.VMEM((n_dp, r, ff), BF16),
            pltpu.VMEM((d, ff), BF16),
            pltpu.VMEM((d, ff), F32),
            pltpu.VMEM((n_dp, n_e, 8, wide_f), BF16),
            pltpu.VMEM((n_dp, 2, d), F32),
            pltpu.VMEM((2, up128(d), 128), F32),
            pltpu.VMEM((1, up128(d)), F32),
            pltpu.VMEM((up128(d), 128), F32),
            dma((6,)), pltpu.SemaphoreType.REGULAR((n_e.bit_length() - 1,)), dma((1,)), dma((4,)),
            dma((n_dp - 1, 2)), dma((n_dp - 1, 4, 2)), dma((n_dp - 1,)), dma((n_dp - 1,)),
            dma((n_dp,)), dma((n_dp,)), dma((n_dp - 1,)), dma((n_dp - 1,)),
        ],
        compiler_params=pltpu.CompilerParams(
            collective_id=0, has_side_effects=True, vmem_limit_bytes=59 * 1024 * 1024),
    )(out_grad.T, routes.reshape(1, tok), pre_act, jnp.swapaxes(out_weight, 1, 2), row_factor,
      col_factor)
    hid, neww, newrow, newcol = pl.pallas_call(
        functools.partial(finish, packed, ff),
        out_shape=tuple(jax.ShapeDtypeStruct(*x) for x in (
            ((tok, ff * n_dp), BF16), ((1, d, ff), BF16), ((1, ff), F32), ((1, d), F32))),
        in_specs=[vm] * 5,
        out_specs=[hbm] * 4,
        scratch_shapes=[pltpu.VMEM((tok, ff * n_dp), BF16), dma((3 + n_dp,))],
        compiler_params=pltpu.CompilerParams(vmem_limit_bytes=8 * 1024 * 1024),
    )(*held)
    return hid, jnp.swapaxes(neww, 1, 2), newrow, newcol


def solution(mesh):
    placed = (
        P(("dp", "expert"), None),
        P(("dp", "expert"), None),
        P(("dp", "expert"), None),
        P("expert", "dp", None),
        P("expert", "dp"),
        P("expert", None),
    )
    return jax.shard_map(
        shards,
        mesh=mesh,
        in_specs=placed,
        out_specs=(
            P(("dp", "expert"), None),
            P("expert", "dp", None),
            P("expert", "dp"),
            P("expert", None),
        ),
        check_vma=False,
    )
```
